32 devices in a mesh: groups: 2 (over y), qring: 4 (over x, core), kvring: 4 (over z), head: 1.
Axes of the slice: x: 2, y: 2, z: 4, core: 2. Of those that a mesh axis runs over, the one named last changes fastest.
Arguments:
- queries: bfloat16 [1536, 4096], P(('groups', 'qring', 'kvring'), 'head'), parts along dimension 0, may hold values from -6 to 6
- keys: bfloat16 [1536, 512], P(('groups', 'qring', 'kvring'), 'head'), parts along dimension 0, may hold values from -6 to 6
- values: bfloat16 [1536, 512], P(('groups', 'qring', 'kvring'), 'head'), parts along dimension 0, may hold values from -6 to 6
- doc_ids: int32 [1536], P('groups'), parts along dimension 0, may hold values from 0 to 15, never falling along the last dimension, each value on 1 to 480 neighbouring positions
- head_mask: int32 [32], P('head'), may hold values 0 or 1
- w_out: bfloat16 [4096, 8192], P('head', 'kvring'), may hold values from -0.5 to 0.5
Outputs:
- mixed: bfloat16 [1536, 8192], P(('groups', 'qring', 'head'), 'kvring'), parts along dimension 0
The draws below stay inside these ranges and needn't reach their ends.
There are 2 independent parts, one for each index of `groups`. The reference program is written for one: setup_inputs(seed, part) draws one part's arguments, and reference() takes and returns one part's arrays. A program takes and returns all parts, laid end to end along the dimension named above; an argument that names none is the same for every part. Nothing has to cross between parts.
All inputs are finite; a program needn't handle non-finite values. No bound on the sum of `head_mask` on one device may be relied on, other than what follows from the above.
Results may differ from the reference program's by a relative error of at most 0.015.
Values may be sent and summed in bfloat16 or wider, within the bound.
A program may use at most 64 MiB of HBM per device.

```python
import math
import jax
import jax.numpy as jnp
import numpy as np
from jax import lax

D = 8192
HEADS = 32
KVH = 4
HD = 128
GROUP = 8
DOCS = 16
SEQ = 768
LONGEST = 480


def draw_queries(key, part):
    base = jnp.clip(1.5 * jax.random.normal(jax.random.fold_in(key, 2), (SEQ, KVH, GROUP, HD), jnp.float32), -6.0, 6.0)
    return base.reshape(SEQ, HEADS * HD).astype(jnp.bfloat16)


def draw_keys(key, part):
    base = jnp.clip(jax.random.normal(jax.random.fold_in(key, 1), (SEQ, KVH, HD), jnp.float32), -6.0, 6.0)
    return base.reshape(SEQ, KVH * HD).astype(jnp.bfloat16)


def plant(drawn, stream_key, low, top_value):
    place = [jax.random.randint(jax.random.fold_in(stream_key, axis), (), 0, length) for axis, length in enumerate(drawn.shape)]
    main_axis = drawn.shape.index(max(drawn.shape))
    next_to = place[:main_axis] + [(place[main_axis] + 1) % drawn.shape[main_axis]] + place[main_axis + 1:]
    return drawn.at[tuple(place)].set(low).at[tuple(next_to)].set(top_value)


def steps_of(rng, extent, pieces, least, high):
    loudness = 1.0
    for axis_at, parts in pieces:
        draws = jax.random.uniform(jax.random.fold_in(jax.random.fold_in(rng, 6), axis_at), (parts,), jnp.float32, least / len(pieces), high / len(pieces))
        loudness = loudness * jnp.repeat(jnp.exp(draws), extent[axis_at] // parts).reshape((-1,) + (1,) * (len(extent) - 1 - axis_at))
    return loudness


def profile(amount, total, most, lean):
    portions = [(1 << 20) // math.isqrt(grade ** lean) + 1 for grade in range(2, amount + 1)]
    spare, holding = total - most - (amount - 1), [1] * (amount - 1)
    while spare > 0:
        free = [i for i in range(amount - 1) if holding[i] < most]
        pool, remaining = sum([portions[i] for i in free]), spare
        for i in free:
            more = min(most - holding[i], max(1, remaining * portions[i] // pool), spare)
            holding[i] = holding[i] + more
            spare = spare - more
    return np.array([most] + holding)


def uneven(key, count, total, most, slope):
    if count == 2:
        one = jax.random.randint(key, (), max(1, total - most), min(most, total - 1) + 1)
        return jnp.stack([one, total - one])
    lengths = jnp.asarray(profile(count, total, most, slope), jnp.int32)
    twos = (count - 1) // 2
    giver, receiver = lengths[1:1 + 2 * twos:2], lengths[2:2 + 2 * twos:2]
    slack = jnp.minimum(giver - 1, most - receiver)
    passed = jax.random.randint(jax.random.fold_in(key, 1), (twos,), 0, 1 << 20) % (slack + 1)
    lengths = lengths.at[1:1 + 2 * twos:2].set(giver - passed).at[2:2 + 2 * twos:2].set(receiver + passed)
    return lengths[jax.random.permutation(jax.random.fold_in(key, 2), count)]


def scatter_about(stream_key, extent, scale, bound, split=(), held_as=jnp.bfloat16):
    array = jax.random.normal(stream_key, extent, jnp.float32) * scale
    if len(split) > 0:
        array = steps_of(stream_key, extent, split, -0.22, 0.18) * array
    return jnp.clip(array, min=-bound, max=bound).astype(held_as)


def setup_inputs(seed: int = 0, part: int = 0) -> dict:
    splits = jax.random.split(jax.random.key(seed), 7)
    part_splits = jax.random.split(jax.random.fold_in(splits[6], part), 7)
    queries = draw_queries(jax.random.fold_in(jax.random.fold_in(splits[6], part), 71), part)
    keys = draw_keys(jax.random.fold_in(jax.random.fold_in(splits[6], part), 71), part)
    values = scatter_about(part_splits[2], (SEQ, KVH * HD), 1.0, 6.0, ((0, 16),))
    doc_ids = jnp.searchsorted(jnp.cumsum(uneven(part_splits[3], DOCS, SEQ, LONGEST, 2)), jnp.arange(SEQ), side="right").astype(jnp.int32)
    head_mask = plant((jax.random.randint(splits[4], (HEADS,), 0, 4) < 3).astype(jnp.int32), jax.random.fold_in(splits[4], 1), 0, 1)
    w_out = scatter_about(splits[5], (HEADS * HD, D), HD ** -0.5, 0.5, ((1, 4),))
    return {"queries": queries, "keys": keys, "values": values, "doc_ids": doc_ids, "head_mask": head_mask, "w_out": w_out}


NEG = -1e+30

def reference(queries, keys, values, doc_ids, head_mask, w_out):
    block_size = math.gcd(SEQ, 256)
    query_all = queries.reshape(SEQ, KVH, GROUP, HD)
    key_all = keys.reshape(SEQ, KVH, HD).astype(jnp.float32)
    value_all = values.reshape(SEQ, KVH, HD).astype(jnp.float32)
    key_pos = jnp.arange(SEQ, dtype=jnp.int32)
    mask_f = head_mask.reshape(KVH, GROUP).astype(jnp.float32)
    scale_factor = 1.0 / math.sqrt(HD)

    def one_block(index):
        start = (index * block_size).astype(jnp.int32)
        query_rows = lax.dynamic_slice_in_dim(query_all, start, block_size, 0).astype(jnp.float32)
        query_doc = lax.dynamic_slice_in_dim(doc_ids, start, block_size, 0)
        query_pos = start + jnp.arange(block_size, dtype=jnp.int32)
        visible = (query_doc[:, None] == doc_ids[None, :]) & (key_pos[None, :] <= query_pos[:, None])
        mask4 = visible[:, None, None, :]
        scores = jnp.einsum('rgec,kgc->rgek', query_rows, key_all) * scale_factor
        scores = jnp.where(mask4, scores, NEG)
        top = lax.optimization_barrier(jnp.max(scores, axis=-1))
        weights = jnp.where(mask4, jnp.exp(scores - top[..., None]), 0.0)
        total = lax.optimization_barrier(jnp.sum(weights, axis=-1))
        rounded = weights.astype(jnp.bfloat16).astype(jnp.float32)
        context = jnp.einsum('rgek,kgc->rgec', rounded, value_all)
        attended = context / total[..., None] * mask_f[None, :, :, None]
        return attended.astype(jnp.bfloat16).reshape(block_size, HEADS * HD)
    blocks = lax.map(one_block, jnp.arange(SEQ // block_size, dtype=jnp.int32))
    attended = blocks.reshape(SEQ, HEADS * HD)
    return jnp.dot(attended, w_out, preferred_element_type=jnp.float32).astype(jnp.bfloat16)
```

```python
import functools
import math

import jax
import jax.numpy as jnp
from jax import lax
from jax.experimental import pallas as pl
from jax.experimental.pallas import tpu as pltpu
from jax.sharding import PartitionSpec as P

HD = 128


NEG = -1e30


def block_rows(total_rows, shard_rows):
    best_size = shard_rows
    for multiple in range(1, total_rows // shard_rows + 1):
        if total_rows // shard_rows % multiple == 0 and multiple * shard_rows <= 256:
            best_size = multiple * shard_rows
    return best_size


def attend_keys(state, visible, queries4, key_rows, value_rows, scale_factor):
    run_max, run_sum, run_out = state
    mask4 = visible[:, None, None, :]
    scores = (
        jnp.einsum("rgec,kgc->rgek", queries4, key_rows, preferred_element_type=jnp.float32)
        * scale_factor
    )
    scores = jnp.where(mask4, scores, NEG)
    new_max = jnp.maximum(run_max, jnp.max(scores, axis=-1))
    weights = jnp.where(mask4, jnp.exp(scores - new_max[..., None]), 0.0)
    shrink = jnp.exp(run_max - new_max)
    run_sum = run_sum * shrink + jnp.sum(weights, axis=-1)
    update = jnp.einsum(
        "rgek,kgc->rgec",
        weights.astype(jnp.bfloat16),
        value_rows,
        preferred_element_type=jnp.float32,
    )
    run_out = run_out * shrink[..., None] + update
    return (new_max, run_sum, run_out)


def fold_piece(
    state, pieces, key_start, queries4, query_doc, query_pos, doc_ids, shard_rows, scale_factor
):
    key_all, value_all = pieces
    total_rows = key_all.shape[0]
    block_size = block_rows(total_rows, shard_rows)

    def one_block(index, carry):
        offset = index * block_size
        key_rows = lax.dynamic_slice_in_dim(key_all, offset, block_size, 0)
        value_rows = lax.dynamic_slice_in_dim(value_all, offset, block_size, 0)
        first = key_start + offset
        key_doc = lax.dynamic_slice_in_dim(doc_ids, first, block_size, 0)
        key_pos = first + jnp.arange(block_size, dtype=jnp.int32)
        visible = (query_doc[:, None] == key_doc[None, :]) & (
            key_pos[None, :] <= query_pos[:, None]
        )
        return attend_keys(carry, visible, queries4, key_rows, value_rows, scale_factor)

    return lax.fori_loop(0, total_rows // block_size, one_block, state)


def per_device(queries, keys, values, doc_ids, head_mask, w_out):
    shard_rows = queries.shape[0]
    kv_local = keys.shape[1] // HD
    q_local = queries.shape[1] // HD
    per_group = q_local // kv_local
    scale_factor = 1.0 / math.sqrt(HD)
    cycle_size = lax.axis_size("kvring")
    cycle_index = lax.axis_index("kvring")
    loop_index = lax.axis_index("qring")
    quarter = cycle_size * shard_rows
    key_rows = keys.reshape(shard_rows, kv_local, HD)
    value_rows = values.reshape(shard_rows, kv_local, HD)
    loop_size = lax.axis_size("qring")
    gathered = lax.all_gather(queries, "qring", axis=0, tiled=True)
    query_total = loop_size * shard_rows
    row_ids = jnp.arange(query_total, dtype=jnp.int32)
    query_pos = row_ids // shard_rows * quarter + cycle_index * shard_rows + row_ids % shard_rows
    queries4 = gathered.reshape(query_total, kv_local, per_group, HD)
    query_doc = jnp.take(doc_ids, query_pos)
    key_base = loop_index * quarter
    initial = (
        jnp.full((query_total, kv_local, per_group), NEG, jnp.float32),
        jnp.zeros((query_total, kv_local, per_group), jnp.float32),
        jnp.zeros((query_total, kv_local, per_group, HD), jnp.float32),
    )
    run_max, run_sum, run_out = fold_piece(
        initial,
        (
            lax.all_gather(key_rows, "kvring", axis=0, tiled=True),
            lax.all_gather(value_rows, "kvring", axis=0, tiled=True),
        ),
        key_base,
        queries4,
        query_doc,
        query_pos,
        doc_ids,
        shard_rows,
        scale_factor,
    )
    top = lax.pmax(run_max, "qring")
    factor = jnp.exp(run_max - top)
    numer, denom = (
        lax.psum_scatter(
            (run_out * factor[..., None]).astype(jnp.bfloat16),
            "qring",
            scatter_dimension=0,
            tiled=True,
        ).astype(jnp.float32),
        lax.psum_scatter(
            (run_sum * factor).astype(jnp.bfloat16), "qring", scatter_dimension=0, tiled=True
        ).astype(jnp.float32),
    )
    mask_f = head_mask.reshape(kv_local, per_group).astype(jnp.float32)
    attended = (
        (numer / denom[..., None] * mask_f[None, :, :, None])
        .astype(jnp.bfloat16)
        .reshape(shard_rows, q_local * HD)
    )
    partial_sum = jnp.dot(
        lax.all_gather(attended, "kvring", axis=0, tiled=True),
        w_out,
        preferred_element_type=jnp.float32,
    )
    return lax.psum_scatter(
        partial_sum.astype(jnp.bfloat16), "head", scatter_dimension=0, tiled=True
    )


LINE = 4
RINGS = 4
CHUNK = 2
STACK = 4
RAW = 4
SLOT_COUNTS = (32,)
VMEM_LIMIT = 62000000


def fused_kernel(
    slot_count,
    per_group,
    doc_hbm,
    mask_hbm,
    q_hbm,
    k_hbm,
    v_hbm,
    w_hbm,
    o_ref,
    doc_row,
    mask_ref,
    next_ref,
    head_ref,
    q_own,
    slots,
    k_all,
    v_all,
    w_all,
    attended,
    bias,
    total,
    local_sem,
    w_sem,
    kv_send,
    kv_recv,
    pass_send,
    mate_send,
    q_send,
    q_recv,
    ready,
):
    z = lax.axis_index("kvring")
    q = lax.axis_index("qring")
    shard = q_hbm.shape[0]
    rows = LINE * shard
    seq = k_all.shape[0]
    head_count = mask_ref.shape[0]
    width = CHUNK * HD
    chunks = slot_count // CHUNK
    raw = min(RAW, chunks)
    w_parts = w_sem.shape[0]
    w_rows = w_hbm.shape[0] // w_parts
    scale2 = math.log2(math.e) / math.sqrt(HD)
    across = lax.rem(q + 2, RINGS)
    mate = q + 1 - 2 * lax.rem(q, 2)
    across_of_mate = lax.rem(mate + 2, RINGS)

    low = q < 2
    high = jnp.logical_not(low)
    even = lax.rem(q, 2) == 0
    quarter = LINE * shard
    upper = z // 2
    sources = (z + 1 - 2 * lax.rem(z, 2), 2 - upper, 3 - 3 * upper)
    middle = (z == 1) | (z == 2)
    end = jnp.logical_not(middle)
    relay_to = (3 - z, sources[0], sources[0])
    has_down = z > 0
    has_up = z < LINE - 1

    def kv_rows(ring_at, line_at):
        return pl.ds(pl.multiple_of((ring_at * LINE + line_at) * shard, 16), shard)

    def q_rows(line_at):
        return pl.ds(pl.multiple_of(line_at * shard, 16), shard)

    def chunk_cols(c):
        return pl.ds(pl.multiple_of(c * width, 128), width)

    def head_cols(head):
        return pl.ds(pl.multiple_of(head * HD, 128), HD)

    def kv_copy(i, from_input, ring_at, line_at, send, target):
        own, everyone = ((k_hbm, k_all), (v_hbm, v_all))[i]
        at = kv_rows(ring_at, line_at)
        return pltpu.make_async_remote_copy(
            src_ref=own if from_input else everyone.at[at],
            dst_ref=everyone.at[at],
            send_sem=send.at[i],
            recv_sem=kv_recv.at[ring_at * LINE + line_at, i],
            device_id=target,
            device_id_type=pl.DeviceIdType.MESH,
        )

    def kv_along(i, line_at):
        return kv_copy(i, True, q, z, kv_send.at[line_at], {"kvring": line_at})

    def kv_arrival(i, ring_at, line_at):
        kv_copy(i, False, ring_at, line_at, kv_send.at[0], {"kvring": sources[0]}).wait_recv()

    def kv_across(i, line_at, place):
        return kv_copy(i, place == 0, q, line_at, pass_send.at[place, 0], {"qring": across})

    def kv_mate(i, line_at, place):
        return kv_copy(i, place == 0, q, line_at, pass_send.at[place, 1], {"qring": mate})

    def kv_on(i, line_at, place):
        return kv_copy(i, False, across, line_at, mate_send.at[place], {"qring": mate})

    def q_copy(line_at, c, kind, target):
        place = slots.at[q_rows(line_at), chunk_cols(c)]
        return pltpu.make_async_remote_copy(
            src_ref=place,
            dst_ref=place,
            send_sem=q_send.at[kind, c],
            recv_sem=q_recv.at[line_at, c],
            device_id={"kvring": target},
            device_id_type=pl.DeviceIdType.MESH,
        )

    def q_arrival(line_at, c):
        q_copy(line_at, c, 0, sources[0]).wait_recv()

    def w_copy(c):
        at = pl.ds(pl.multiple_of(c * w_rows, 128), w_rows)
        return pltpu.make_async_copy(w_hbm.at[at], w_all.at[at], w_sem.at[c])

    local = [
        pltpu.make_async_copy(mask_hbm, mask_ref, local_sem.at[0]),
        pltpu.make_async_copy(q_hbm, q_own, local_sem.at[1]),
        pltpu.make_async_copy(doc_hbm, doc_row, local_sem.at[2]),
        pltpu.make_async_copy(k_hbm, k_all.at[kv_rows(q, z)], local_sem.at[3]),
        pltpu.make_async_copy(v_hbm, v_all.at[kv_rows(q, z)], local_sem.at[4]),
    ]

    for copy in local:
        copy.start()

    barrier = pltpu.get_barrier_semaphore()
    for step in range(1, LINE):

        @pl.when(z + step < LINE)
        def _(step=step):
            pl.semaphore_signal(
                barrier, inc=1, device_id={"kvring": z + step}, device_id_type=pl.DeviceIdType.MESH
            )

    for ring_at in (across, mate):
        pl.semaphore_signal(
            barrier, inc=1, device_id={"qring": ring_at}, device_id_type=pl.DeviceIdType.MESH
        )
    pl.semaphore_wait(barrier, z + 2)
    for step in range(1, LINE):

        @pl.when(z >= step)
        def _(step=step):
            pl.semaphore_signal(
                ready.at[z], inc=1, device_id={"kvring": z - step}, device_id_type=pl.DeviceIdType.MESH
            )

    for step in range(1, LINE):

        @pl.when(z >= step)
        def _(step=step):
            for i in range(2):
                kv_along(i, z - step).start()

    def pass_on(i, line_at, place):
        @pl.when(low)
        def _():
            kv_across(i, line_at, place).start()

        @pl.when(even)
        def _():
            kv_mate(i, line_at, place).start()

    def pass_across_on(i, line_at, place):
        @pl.when(high)
        def _():
            kv_arrival(i, across, line_at)
            kv_on(i, line_at, place).start()

    for i in range(2):
        pass_on(i, z, 0)

    for later in range(1, RINGS):

        @pl.when(q < later)
        def _(later=later):
            at = slice(later * quarter, (later + 1) * quarter)
            k_all[at] = jnp.zeros((quarter, k_all.shape[1]), k_all.dtype)
            v_all[at] = jnp.zeros((quarter, v_all.shape[1]), v_all.dtype)

    lag = head_count - slot_count
    local[0].wait()

    later = dropped = jnp.int32(0)
    later = later + head_count
    next_ref[head_count] = later
    for head in reversed(range(head_count)):
        drop = jnp.where(dropped < lag, 1 - mask_ref[head], 0)
        later = head + drop * (later - head)
        dropped = dropped + drop
        next_ref[head] = later
    for s in range(slot_count):
        head_ref[s] = later
        later = next_ref[jnp.minimum(later + 1, head_count)]

    def slot_head(s):
        return jnp.minimum(head_ref[s], head_count - 1)

    def slot_keep(s):
        return mask_ref[slot_head(s)].astype(jnp.float32)

    local[1].wait()

    @pl.loop(0, raw)
    def _(c):
        for e in range(CHUNK):
            s = c * CHUNK + e
            slots[q_rows(z), head_cols(s)] = q_own[:, head_cols(slot_head(s))]

        @pl.when(has_down)
        def _():
            q_copy(z, c, 0, z - 1).start()

    for step in range(1, LINE):

        @pl.when(z + step < LINE)
        def _(step=step):
            pl.semaphore_wait(ready.at[z + step], 1)
            for i in range(2):
                kv_along(i, z + step).start()

    @pl.when(has_up)
    def _():
        @pl.loop(0, raw)
        def _(c):
            q_copy(z, c, 1, z + 1).start()

    @pl.loop(0, w_parts)
    def _(c):
        w_copy(c).start()

    def relay(i, c):
        @pl.when(middle)
        def _():
            q_arrival(sources[i], c)
            q_copy(sources[i], c, 2 + i, relay_to[i]).start()

    def arrive(c):
        @pl.when(end)
        def _():
            for line_at in sources:
                q_arrival(line_at, c)

    places = (z,) + sources
    for place, line_at in enumerate(sources):
        for i in range(2):
            kv_arrival(i, q, line_at)
            pass_on(i, line_at, place + 1)
        for i in range(2):
            pass_across_on(i, places[place], place)

    @pl.loop(0, raw)
    def _(c):
        relay(0, c)
        relay(1, c)

    local[2].wait()
    row_at = q * rows + lax.broadcasted_iota(jnp.int32, (rows, seq), 0)
    key_at = lax.broadcasted_iota(jnp.int32, (rows, seq), 1)
    key_doc = jnp.broadcast_to(doc_row[...].reshape(1, seq), (rows, seq))
    row_doc = jnp.sum(jnp.where(row_at == key_at, key_doc, 0), axis=1, keepdims=True)
    bias[...] = jnp.where((key_doc == row_doc) & (key_at <= row_at), 0.0, NEG)
    for i in range(2):
        pass_across_on(i, sources[2], 3)
    for copy in local[3:]:
        copy.wait()

    @pl.when(high | (q == 1))
    def _():
        for line_at in places:
            for i in range(2):
                kv_arrival(i, jnp.where(q == 2, 1, 0), line_at)

    @pl.when(q == 3)
    def _():
        for line_at in places:
            for i in range(2):
                kv_arrival(i, mate, line_at)

    def attend(queries, hidden, kv_head):
        kv_cols = head_cols(kv_head)
        scores = lax.dot_general(
            queries, k_all[:, kv_cols], (((1,), (1,)), ((), ())), preferred_element_type=jnp.float32
        )
        parts = queries.shape[0] // hidden.shape[0]
        scores = (scores * scale2).reshape(parts, hidden.shape[0], seq) + hidden[None]
        scores = scores.reshape(queries.shape[0], seq)
        top = jnp.max(scores, axis=-1, keepdims=True)
        weights = jnp.exp2(scores - top)
        denom = jnp.sum(weights, axis=-1, keepdims=True)
        context = jnp.dot(
            weights.astype(jnp.bfloat16), v_all[:, kv_cols], preferred_element_type=jnp.float32
        )
        return context / denom

    def send(c):
        @pl.when(has_down)
        def _():
            q_copy(z, c, 0, z - 1).start()

        @pl.when(has_up)
        def _():
            q_copy(z, c, 1, z + 1).start()

    start = raw * CHUNK // STACK
    groups = head_count // STACK

    @pl.loop(start, groups)
    def _(g):
        heads = [g * STACK + e for e in range(STACK)]
        stacked = jnp.concatenate([q_own[:, head_cols(head)] for head in heads], axis=0)
        result = attend(stacked, bias[q_rows(z), :], g * STACK // per_group)
        for e, head in enumerate(heads):
            q_own[:, head_cols(head)] = result[e * shard : (e + 1) * shard].astype(jnp.bfloat16)
        for k in range(STACK // CHUNK):
            c = (g * STACK - lag) // CHUNK + k

            @pl.when(c >= raw)
            def _(c=c):
                for e in range(CHUNK):
                    s = c * CHUNK + e
                    block = q_own[:, head_cols(slot_head(s))].astype(jnp.float32) * slot_keep(s)
                    slots[q_rows(z), head_cols(s)] = block.astype(jnp.bfloat16)
                send(c)

        @pl.when(g - start < raw)
        def _():
            relay(2, g - start)

    for c in range(groups - start, raw):
        relay(2, c)

    @pl.loop(0, w_parts)
    def _(c):
        w_copy(c).wait()

    def project(block, c, count):
        weights = jnp.concatenate(
            [
                w_all[pl.ds(pl.multiple_of(slot_head(c * CHUNK + e) * HD, HD), HD), :]
                for e in range(count * CHUNK)
            ],
            axis=0,
        )
        return jnp.dot(block, weights, preferred_element_type=jnp.float32)

    per_step = -(-(chunks - raw) // raw)

    @pl.loop(0, raw)
    def _(c):
        arrive(c)
        for e in range(CHUNK):
            s = c * CHUNK + e
            head = slot_head(s)
            result = attend(slots[:, head_cols(s)], bias[...], head // per_group)
            attended[:, head_cols(s)] = (result * slot_keep(s)).astype(jnp.bfloat16)
        for k in range(per_step):
            ahead = raw + c * per_step + k

            @pl.when(ahead < chunks)
            def _(ahead=ahead):
                relay(0, ahead)
                relay(1, ahead)

    def wide_cols(c, count):
        return pl.ds(pl.multiple_of(c * width, 128), count * width)

    total[...] = project(attended[:, : 2 * width], 0, 2)
    for c in range(2, raw, 2):
        count = min(2, raw - c)
        total[...] += project(attended[:, c * width : (c + count) * width], c, count)

    def take(c, count):
        for k in range(count):
            arrive(c + k)
            relay(2, c + k)
        total[...] += project(slots[:, wide_cols(c, count)], c, count)

    odd = (chunks - raw) % 2
    if odd:
        take(raw, 1)

    @pl.loop(0, (chunks - raw - odd) // 2)
    def _(pair):
        take(raw + odd + 2 * pair, 2)

    o_ref[...] = total[...].astype(jnp.bfloat16)

    for line_at in sources:
        for i in range(2):
            kv_along(i, line_at).wait_send()

    @pl.when(has_down)
    def _():
        @pl.loop(0, chunks)
        def _(c):
            q_copy(z, c, 0, z - 1).wait_send()

    @pl.when(has_up)
    def _():
        @pl.loop(0, chunks)
        def _(c):
            q_copy(z, c, 1, z + 1).wait_send()

    @pl.when(middle)
    def _():
        for i, line_at in enumerate(sources):

            @pl.loop(0, chunks)
            def _(c, i=i, line_at=line_at):
                q_copy(line_at, c, 2 + i, relay_to[i]).wait_send()

    for place, line_at in enumerate(places):
        for i in range(2):

            @pl.when(low)
            def _(i=i, place=place, line_at=line_at):
                kv_across(i, line_at, place).wait_send()

            @pl.when(even)
            def _(i=i, place=place, line_at=line_at):
                kv_mate(i, line_at, place).wait_send()

            @pl.when(high)
            def _(i=i, place=place, line_at=line_at):
                kv_on(i, line_at, place).wait_send()


def write_kernel(held, out, sem):
    parts = sem.shape[0]
    size = held.shape[0] // parts
    copies = []
    for i in range(parts):
        at = pl.ds(i * size, size)
        copies.append(pltpu.make_async_copy(held.at[at], out.at[at], sem.at[i]))
    for copy in copies:
        copy.start()
    for copy in copies:
        copy.wait()


def fused_call(variant, doc_ids, head_mask, queries, keys, values, w_out):
    slot_count = SLOT_COUNTS[variant]
    shard_rows = queries.shape[0]
    seq = doc_ids.shape[0]
    rows = LINE * shard_rows
    columns = w_out.shape[1]
    heads = head_mask.shape[0]
    chunks = slot_count // CHUNK
    width = CHUNK * HD
    per_group = queries.shape[1] // keys.shape[1]
    anywhere = pl.BlockSpec(memory_space=pl.ANY)
    dma = pltpu.SemaphoreType.DMA
    return pl.pallas_call(
        functools.partial(fused_kernel, slot_count, per_group),
        out_shape=pltpu.VMEM((rows, columns), jnp.bfloat16),
        in_specs=[anywhere] * 6,
        out_specs=pl.BlockSpec(memory_space=pltpu.VMEM),
        scratch_shapes=[
            pltpu.VMEM((seq,), jnp.int32),
            pltpu.SMEM((heads,), jnp.int32),
            pltpu.SMEM((heads + 1,), jnp.int32),
            pltpu.SMEM((slot_count,), jnp.int32),
            pltpu.VMEM(queries.shape, jnp.bfloat16),
            pltpu.VMEM((rows, slot_count * HD), jnp.bfloat16),
            pltpu.VMEM((seq, keys.shape[1]), jnp.bfloat16),
            pltpu.VMEM((seq, keys.shape[1]), jnp.bfloat16),
            pltpu.VMEM(w_out.shape, jnp.bfloat16),
            pltpu.VMEM((rows, min(RAW, chunks) * width), jnp.bfloat16),
            pltpu.VMEM((rows, seq), jnp.float32),
            pltpu.VMEM((rows, columns), jnp.float32),
            dma((5,)),
            dma((8,)),
            dma((LINE, 2)),
            dma((RINGS * LINE, 2)),
            dma((LINE, 2, 2)),
            dma((LINE, 2)),
            dma((5, chunks)),
            dma((LINE, chunks)),
            pltpu.SemaphoreType.REGULAR((LINE,)),
        ],
        compiler_params=pltpu.CompilerParams(
            collective_id=variant, has_side_effects=True, vmem_limit_bytes=VMEM_LIMIT
        ),
    )(doc_ids, head_mask, queries, keys, values, w_out)


def fused_device(queries, keys, values, doc_ids, head_mask, w_out):
    operands = (doc_ids, head_mask, queries, keys, values, w_out)
    if len(SLOT_COUNTS) == 1:
        held = fused_call(0, *operands)
    else:
        shift = CHUNK.bit_length() - 1
        above = lax.reduce(head_mask, jnp.int32(CHUNK - 1 - SLOT_COUNTS[0]), lax.add, (0,))
        which = lax.shift_right_arithmetic(above, jnp.int32(shift))
        held = lax.switch(
            which, [functools.partial(fused_call, i) for i in range(len(SLOT_COUNTS))], *operands
        )
    return pl.pallas_call(
        write_kernel,
        out_shape=jax.ShapeDtypeStruct(held.shape, held.dtype),
        in_specs=[pl.BlockSpec(memory_space=pltpu.VMEM)],
        out_specs=pl.BlockSpec(memory_space=pl.ANY),
        scratch_shapes=[pltpu.SemaphoreType.DMA((4,))],
        compiler_params=pltpu.CompilerParams(vmem_limit_bytes=8 << 20),
    )(held)


def solution(mesh):
    sizes = (mesh.shape["qring"], mesh.shape["kvring"], mesh.shape["head"])
    small = sizes == (RINGS, LINE, 1)
    placed = (
        P(("groups", "qring", "kvring"), "head"),
        P(("groups", "qring", "kvring"), "head"),
        P(("groups", "qring", "kvring"), "head"),
        P("groups"),
        P("head"),
        P("head", "kvring"),
    )
    return jax.shard_map(
        fused_device if small else per_device,
        mesh=mesh,
        in_specs=placed,
        out_specs=P(("groups", "qring", "head"), "kvring"),
        check_vma=False,
    )
```

```python
import functools
import math

import jax
import jax.numpy as jnp
from jax import lax
from jax.experimental import pallas as pl
from jax.experimental.pallas import tpu as pltpu
from jax.sharding import PartitionSpec as P

HD = 128


NEG = -1e30


def block_rows(total_rows, shard_rows):
    best_size = shard_rows
    for multiple in range(1, total_rows // shard_rows + 1):
        if total_rows // shard_rows % multiple == 0 and multiple * shard_rows <= 256:
            best_size = multiple * shard_rows
    return best_size


def attend_keys(state, visible, queries4, key_rows, value_rows, scale_factor):
    run_max, run_sum, run_out = state
    mask4 = visible[:, None, None, :]
    scores = (
        jnp.einsum("rgec,kgc->rgek", queries4, key_rows, preferred_element_type=jnp.float32)
        * scale_factor
    )
    scores = jnp.where(mask4, scores, NEG)
    new_max = jnp.maximum(run_max, jnp.max(scores, axis=-1))
    weights = jnp.where(mask4, jnp.exp(scores - new_max[..., None]), 0.0)
    shrink = jnp.exp(run_max - new_max)
    run_sum = run_sum * shrink + jnp.sum(weights, axis=-1)
    update = jnp.einsum(
        "rgek,kgc->rgec",
        weights.astype(jnp.bfloat16),
        value_rows,
        preferred_element_type=jnp.float32,
    )
    run_out = run_out * shrink[..., None] + update
    return (new_max, run_sum, run_out)


def fold_piece(
    state, pieces, key_start, queries4, query_doc, query_pos, doc_ids, shard_rows, scale_factor
):
    key_all, value_all = pieces
    total_rows = key_all.shape[0]
    block_size = block_rows(total_rows, shard_rows)

    def one_block(index, carry):
        offset = index * block_size
        key_rows = lax.dynamic_slice_in_dim(key_all, offset, block_size, 0)
        value_rows = lax.dynamic_slice_in_dim(value_all, offset, block_size, 0)
        first = key_start + offset
        key_doc = lax.dynamic_slice_in_dim(doc_ids, first, block_size, 0)
        key_pos = first + jnp.arange(block_size, dtype=jnp.int32)
        visible = (query_doc[:, None] == key_doc[None, :]) & (
            key_pos[None, :] <= query_pos[:, None]
        )
        return attend_keys(carry, visible, queries4, key_rows, value_rows, scale_factor)

    return lax.fori_loop(0, total_rows // block_size, one_block, state)


def per_device(queries, keys, values, doc_ids, head_mask, w_out):
    shard_rows = queries.shape[0]
    kv_local = keys.shape[1] // HD
    q_local = queries.shape[1] // HD
    per_group = q_local // kv_local
    scale_factor = 1.0 / math.sqrt(HD)
    cycle_size = lax.axis_size("kvring")
    cycle_index = lax.axis_index("kvring")
    loop_index = lax.axis_index("qring")
    quarter = cycle_size * shard_rows
    key_rows = keys.reshape(shard_rows, kv_local, HD)
    value_rows = values.reshape(shard_rows, kv_local, HD)
    loop_size = lax.axis_size("qring")
    gathered = lax.all_gather(queries, "qring", axis=0, tiled=True)
    query_total = loop_size * shard_rows
    row_ids = jnp.arange(query_total, dtype=jnp.int32)
    query_pos = row_ids // shard_rows * quarter + cycle_index * shard_rows + row_ids % shard_rows
    queries4 = gathered.reshape(query_total, kv_local, per_group, HD)
    query_doc = jnp.take(doc_ids, query_pos)
    key_base = loop_index * quarter
    initial = (
        jnp.full((query_total, kv_local, per_group), NEG, jnp.float32),
        jnp.zeros((query_total, kv_local, per_group), jnp.float32),
        jnp.zeros((query_total, kv_local, per_group, HD), jnp.float32),
    )
    run_max, run_sum, run_out = fold_piece(
        initial,
        (
            lax.all_gather(key_rows, "kvring", axis=0, tiled=True),
            lax.all_gather(value_rows, "kvring", axis=0, tiled=True),
        ),
        key_base,
        queries4,
        query_doc,
        query_pos,
        doc_ids,
        shard_rows,
        scale_factor,
    )
    top = lax.pmax(run_max, "qring")
    factor = jnp.exp(run_max - top)
    numer, denom = (
        lax.psum_scatter(
            (run_out * factor[..., None]).astype(jnp.bfloat16),
            "qring",
            scatter_dimension=0,
            tiled=True,
        ).astype(jnp.float32),
        lax.psum_scatter(
            (run_sum * factor).astype(jnp.bfloat16), "qring", scatter_dimension=0, tiled=True
        ).astype(jnp.float32),
    )
    mask_f = head_mask.reshape(kv_local, per_group).astype(jnp.float32)
    attended = (
        (numer / denom[..., None] * mask_f[None, :, :, None])
        .astype(jnp.bfloat16)
        .reshape(shard_rows, q_local * HD)
    )
    partial_sum = jnp.dot(
        lax.all_gather(attended, "kvring", axis=0, tiled=True),
        w_out,
        preferred_element_type=jnp.float32,
    )
    return lax.psum_scatter(
        partial_sum.astype(jnp.bfloat16), "head", scatter_dimension=0, tiled=True
    )


LINE = 4
RINGS = 4
CHUNK = 2
STACK = 4
RAW = 4
SLOT_COUNTS = tuple(range(16, 33, 2))
VMEM_LIMIT = 62000000


def fused_kernel(
    slot_count,
    per_group,
    doc_hbm,
    mask_hbm,
    q_hbm,
    k_hbm,
    v_hbm,
    w_hbm,
    o_ref,
    doc_row,
    mask_ref,
    next_ref,
    head_ref,
    q_own,
    q_heads,
    slots,
    kv_all,
    w_all,
    attended,
    bias,
    total,
    local_sem,
    own_sem,
    w_sem,
    kv_send,
    kv_recv,
    kv_pass,
    pass_send,
    mate_send,
    q_send,
    q_recv,
    ready,
):
    z = lax.axis_index("kvring")
    q = lax.axis_index("qring")
    shard = q_hbm.shape[0]
    rows = LINE * shard
    kv_count, _, seq, _ = kv_all.shape
    kv_order = tuple(range(1, kv_count)) + (0,)
    head_count = mask_ref.shape[0]
    width = CHUNK * HD
    chunks = slot_count // CHUNK
    raw = min(RAW, chunks)
    scale2 = math.log2(math.e) / math.sqrt(HD)
    across = lax.rem(q + 2, RINGS)
    mate = q + 1 - 2 * lax.rem(q, 2)
    across_of_mate = lax.rem(mate + 2, RINGS)

    low = q < 2
    high = jnp.logical_not(low)
    even = lax.rem(q, 2) == 0
    quarter = LINE * shard
    upper = z // 2
    sources = (z + 1 - 2 * lax.rem(z, 2), 2 - upper, 3 - 3 * upper)
    middle = (z == 1) | (z == 2)
    end = jnp.logical_not(middle)
    side = sources[0]

    def kv_rows(ring_at, line_at):
        return pl.ds(pl.multiple_of((ring_at * LINE + line_at) * shard, 16), shard)

    def q_rows(line_at):
        return pl.ds(pl.multiple_of(line_at * shard, 16), shard)

    def chunk_cols(c):
        return pl.ds(pl.multiple_of(c * width, 128), width)

    def head_cols(head):
        return pl.ds(pl.multiple_of(head * HD, 128), HD)

    def kv_copy(g, ring_at, line_at, send, target):
        place = kv_all.at[g, :, kv_rows(ring_at, line_at)]
        return pltpu.make_async_remote_copy(
            src_ref=place,
            dst_ref=place,
            send_sem=send.at[g],
            recv_sem=kv_recv.at[ring_at * LINE + line_at, g],
            device_id=target,
            device_id_type=pl.DeviceIdType.MESH,
        )

    def kv_along(g, line_at):
        return kv_copy(g, q, z, kv_send.at[line_at], {"kvring": line_at})

    def kv_arrival(g, ring_at, line_at):
        kv_copy(g, ring_at, line_at, kv_send.at[0], {"kvring": side}).wait_recv()

    def kv_across(g, line_at, place):
        return kv_copy(g, q, line_at, pass_send.at[place, 0], {"qring": across})

    def kv_mate(g, line_at, place):
        return kv_copy(g, q, line_at, pass_send.at[place, 1], {"qring": mate})

    def kv_on(g, line_at, place):
        return kv_copy(g, across, line_at, mate_send.at[place], {"qring": mate})

    def q_copy(line_at, c, kind, target):
        place = slots.at[q_rows(line_at), chunk_cols(c)]
        return pltpu.make_async_remote_copy(
            src_ref=place,
            dst_ref=place,
            send_sem=q_send.at[kind, c],
            recv_sem=q_recv.at[line_at, c],
            device_id={"kvring": target},
            device_id_type=pl.DeviceIdType.MESH,
        )

    def send_chunk(c, line_at):
        q_copy(z, c, line_at, line_at).start()

    def q_arrival(line_at, c):
        q_copy(line_at, c, 0, side).wait_recv()

    def w_copy(head):
        at = pl.ds(pl.multiple_of(head * HD, HD), HD)
        return pltpu.make_async_copy(w_hbm.at[at], w_all.at[head], w_sem.at[head])

    local = [
        pltpu.make_async_copy(mask_hbm, mask_ref, local_sem.at[0]),
        pltpu.make_async_copy(q_hbm, q_own, local_sem.at[1]),
        pltpu.make_async_copy(doc_hbm, doc_row, local_sem.at[2]),
    ]
    own_kv = []
    for g in kv_order:
        for i, own in enumerate((k_hbm, v_hbm)):
            at = kv_all.at[g, i, kv_rows(q, z)]
            own_kv.append(pltpu.make_async_copy(own.at[:, g * HD : (g + 1) * HD], at, own_sem.at[g, i]))

    for copy in own_kv + local:
        copy.start()

    barrier = pltpu.get_barrier_semaphore()
    for step in (1, 2):

        @pl.when(z + step < LINE)
        def _(step=step):
            pl.semaphore_signal(
                barrier, inc=1, device_id={"kvring": z + step}, device_id_type=pl.DeviceIdType.MESH
            )

    for ring_at in (across, mate):
        pl.semaphore_signal(
            barrier, inc=1, device_id={"qring": ring_at}, device_id_type=pl.DeviceIdType.MESH
        )
    pl.semaphore_wait(barrier, jnp.minimum(z, 2) + 2)
    def tell(line_at):
        pl.semaphore_signal(
            ready.at[z], inc=1, device_id={"kvring": line_at}, device_id_type=pl.DeviceIdType.MESH
        )

    @pl.when(z > 0)
    def _():
        tell(z - 1)

    @pl.when(z == 2)
    def _():
        tell(0)

    def down(send):
        @pl.when(z == LINE - 1)
        def _():
            send(z - 2)

        @pl.when(z > 0)
        def _():
            send(z - 1)

    def up(send):
        @pl.when(z == 0)
        def _():
            send(z + 2)

        @pl.when(z < LINE - 1)
        def _():
            send(z + 1)

    def send_kv(line_at):
        for g in kv_order:
            kv_along(g, line_at).start()

    for copy in own_kv:
        copy.wait()
    down(send_kv)

    def pass_on(g, line_at, place):
        @pl.when(low)
        def _():
            kv_across(g, line_at, place).start()

        @pl.when(even)
        def _():
            kv_mate(g, line_at, place).start()

    for g in kv_order:
        pass_on(g, z, 0)

    lag = head_count - slot_count
    local[0].wait()

    later = dropped = jnp.int32(0)
    later = later + head_count
    next_ref[head_count] = later
    for head in reversed(range(head_count)):
        drop = jnp.where(dropped < lag, 1 - mask_ref[head], 0)
        later = head + drop * (later - head)
        dropped = dropped + drop
        next_ref[head] = later
    for s in range(slot_count):
        head_ref[s] = later
        later = next_ref[jnp.minimum(later + 1, head_count)]

    def slot_head(s):
        return jnp.minimum(head_ref[s], head_count - 1)

    def slot_keep(s):
        return mask_ref[slot_head(s)].astype(jnp.float32)

    local[1].wait()
    for head in range(head_count):
        q_heads[head] = q_own[:, head * HD : (head + 1) * HD]

    @pl.loop(0, raw)
    def _(c):
        for e in range(CHUNK):
            s = c * CHUNK + e
            slots[q_rows(z), head_cols(s)] = q_heads[slot_head(s)]

        down(functools.partial(send_chunk, c))

    @pl.when(z < LINE - 1)
    def _():
        pl.semaphore_wait(ready.at[z + 1], 1)
        send_kv(z + 1)

    @pl.when(z == 0)
    def _():
        pl.semaphore_wait(ready.at[2], 1)
        send_kv(2)

    @pl.loop(0, raw)
    def _(c):
        up(functools.partial(send_chunk, c))

    for later in range(1, RINGS):

        @pl.when(q < later)
        def _(later=later):
            at = slice(later * quarter, (later + 1) * quarter)
            kv_all[:, :, at] = jnp.zeros((kv_count, 2, quarter, HD), kv_all.dtype)

    @pl.loop(0, head_count)
    def _(c):
        w_copy(c).start()

    def relay(i, c):
        @pl.when(middle)
        def _():
            q_arrival(sources[i], c)
            q_copy(sources[i], c, LINE - 1 + i, side).start()

    def kv_relay(g, place):
        return kv_copy(g, q, sources[place], kv_pass.at[place - 1], {"kvring": side})

    def near(c):
        @pl.when(middle)
        def _():
            q_arrival(side, c)

    def arrive(c):
        @pl.when(end)
        def _():
            for line_at in sources:
                q_arrival(line_at, c)

    places = (z,) + sources

    def kv_from_line(g):
        for place, line_at in enumerate(sources):
            kv_arrival(g, q, line_at)
            if place > 0:

                @pl.when(middle)
                def _(place=place):
                    kv_relay(g, place).start()

            pass_on(g, line_at, place + 1)

    def kv_from_across(g):
        @pl.when(high)
        def _():
            for place, line_at in enumerate(places):
                kv_arrival(g, across, line_at)
                kv_on(g, line_at, place).start()

    def kv_from_mate(g):
        @pl.when(q > 0)
        def _():
            for line_at in places:
                kv_arrival(g, jnp.where(q == 2, 1, 0), line_at)

        @pl.when(q == 3)
        def _():
            for line_at in places:
                kv_arrival(g, mate, line_at)

    local[2].wait()
    row_at = q * rows + lax.broadcasted_iota(jnp.int32, (rows, seq), 0)
    key_at = lax.broadcasted_iota(jnp.int32, (rows, seq), 1)
    key_doc = jnp.broadcast_to(doc_row[...].reshape(1, seq), (rows, seq))
    row_doc = jnp.sum(jnp.where(row_at == key_at, key_doc, 0), axis=1, keepdims=True)
    bias[...] = jnp.where((key_doc == row_doc) & (key_at <= row_at), 0.0, NEG)

    def attend(queries, hidden, key_block, value_block):
        scores = lax.dot_general(
            queries, key_block, (((1,), (1,)), ((), ())), preferred_element_type=jnp.float32
        )
        parts = queries.shape[0] // hidden.shape[0]
        scores = (scores * scale2).reshape(parts, hidden.shape[0], seq) + hidden[None]
        scores = scores.reshape(queries.shape[0], seq)
        top = jnp.max(scores, axis=-1, keepdims=True)
        weights = jnp.exp2(scores - top)
        denom = jnp.sum(weights, axis=-1, keepdims=True)
        context = jnp.dot(
            weights.astype(jnp.bfloat16), value_block, preferred_element_type=jnp.float32
        )
        return context / denom

    def own_stack(g):
        heads = [g * STACK + e for e in range(STACK)]
        stacked = jnp.concatenate([q_heads[head] for head in heads], axis=0)
        kv_head = g * STACK // per_group
        result = attend(stacked, bias[q_rows(z), :], kv_all[kv_head, 0], kv_all[kv_head, 1])
        for e, head in enumerate(heads):
            q_heads[head] = result[e * shard : (e + 1) * shard].astype(jnp.bfloat16)
        for k in range(STACK // CHUNK):
            c = (g * STACK - lag) // CHUNK + k

            @pl.when(c >= raw)
            def _(c=c):
                for e in range(CHUNK):
                    s = c * CHUNK + e
                    block = q_heads[slot_head(s)].astype(jnp.float32) * slot_keep(s)
                    slots[q_rows(z), head_cols(s)] = block.astype(jnp.bfloat16)
                down(functools.partial(send_chunk, c))
                up(functools.partial(send_chunk, c))

    def own_heads(g):
        pl.loop(g * per_group // STACK, (g + 1) * per_group // STACK)(own_stack)

    def raw_relays(i):
        @pl.loop(0, raw)
        def _(c):
            relay(i, c)

    last = len(kv_order) - 1
    kv_from_line(kv_order[0])
    for t, g in enumerate(kv_order):
        if t < last:
            kv_from_line(kv_order[t + 1])
        kv_from_across(g)
        if t == 1:
            raw_relays(1)
        if t == 2:
            raw_relays(2)
        if t > 0:
            kv_from_mate(kv_order[t - 1])
            own_heads(kv_order[t - 1])
    kv_from_mate(kv_order[last])

    @pl.loop(0, head_count)
    def _(c):
        w_copy(c).wait()

    def project(block, c, count):
        weights = jnp.concatenate(
            [
                w_all[slot_head(c * CHUNK + e)]
                for e in range(count * CHUNK)
            ],
            axis=0,
        )
        return jnp.dot(block, weights, preferred_element_type=jnp.float32)

    per_step = -(-(chunks - raw) // raw)

    @pl.loop(0, raw)
    def _(c):
        arrive(c)
        near(c)
        for e in range(CHUNK):
            s = c * CHUNK + e
            kv_head = slot_head(s) // per_group
            result = attend(slots[:, head_cols(s)], bias[...], kv_all[kv_head, 0], kv_all[kv_head, 1])
            attended[:, head_cols(s)] = (result * slot_keep(s)).astype(jnp.bfloat16)
        for k in range(per_step):
            ahead = raw + c * per_step + k

            @pl.when(ahead < chunks)
            def _(ahead=ahead):
                relay(1, ahead)

    def wide_cols(c, count):
        return pl.ds(pl.multiple_of(c * width, 128), count * width)

    total[...] = project(attended[:, : 2 * width], 0, 2)
    for c in range(2, raw, 2):
        count = min(2, raw - c)
        total[...] += project(attended[:, c * width : (c + count) * width], c, count)

    def take(c, count):
        for k in range(count):
            arrive(c + k)
            near(c + k)
            relay(2, c + k)
        total[...] += project(slots[:, wide_cols(c, count)], c, count)

    odd = (chunks - raw) % 2
    if odd:
        take(raw, 1)

    @pl.loop(0, (chunks - raw - odd) // 2)
    def _(pair):
        take(raw + odd + 2 * pair, 2)

    o_ref[...] = total[...].astype(jnp.bfloat16)

    def sent(line_at):
        for g in kv_order:
            kv_along(g, line_at).wait_send()

        @pl.loop(0, chunks)
        def _(c):
            q_copy(z, c, line_at, line_at).wait_send()

    down(sent)
    up(sent)

    @pl.when(middle)
    def _():
        for place in (1, 2):
            for g in kv_order:
                kv_relay(g, place).wait_send()

            @pl.loop(0, chunks)
            def _(c, place=place):
                q_copy(sources[place], c, LINE - 1 + place, side).wait_send()

    for place, line_at in enumerate(places):
        for g in kv_order:

            @pl.when(low)
            def _(g=g, place=place, line_at=line_at):
                kv_across(g, line_at, place).wait_send()

            @pl.when(even)
            def _(g=g, place=place, line_at=line_at):
                kv_mate(g, line_at, place).wait_send()

            @pl.when(high)
            def _(g=g, place=place, line_at=line_at):
                kv_on(g, line_at, place).wait_send()


def write_kernel(held, out, sem):
    parts = sem.shape[0]
    size = held.shape[0] // parts
    copies = []
    for i in range(parts):
        at = pl.ds(i * size, size)
        copies.append(pltpu.make_async_copy(held.at[at], out.at[at], sem.at[i]))
    for copy in copies:
        copy.start()
    for copy in copies:
        copy.wait()


def fused_call(variant, doc_ids, head_mask, queries, keys, values, w_out):
    slot_count = SLOT_COUNTS[variant]
    shard_rows = queries.shape[0]
    seq = doc_ids.shape[0]
    rows = LINE * shard_rows
    columns = w_out.shape[1]
    heads = head_mask.shape[0]
    chunks = slot_count // CHUNK
    width = CHUNK * HD
    kv_heads = keys.shape[1] // HD
    per_group = heads // kv_heads
    anywhere = pl.BlockSpec(memory_space=pl.ANY)
    dma = pltpu.SemaphoreType.DMA
    return pl.pallas_call(
        functools.partial(fused_kernel, slot_count, per_group),
        out_shape=pltpu.VMEM((rows, columns), jnp.bfloat16),
        in_specs=[anywhere] * 6,
        out_specs=pl.BlockSpec(memory_space=pltpu.VMEM),
        scratch_shapes=[
            pltpu.VMEM((seq,), jnp.int32),
            pltpu.SMEM((heads,), jnp.int32),
            pltpu.SMEM((heads + 1,), jnp.int32),
            pltpu.SMEM((slot_count,), jnp.int32),
            pltpu.VMEM(queries.shape, jnp.bfloat16),
            pltpu.VMEM((heads, shard_rows, HD), jnp.bfloat16),
            pltpu.VMEM((rows, slot_count * HD), jnp.bfloat16),
            pltpu.VMEM((kv_heads, 2, seq, HD), jnp.bfloat16),
            pltpu.VMEM((heads, HD, columns), jnp.bfloat16),
            pltpu.VMEM((rows, min(RAW, chunks) * width), jnp.bfloat16),
            pltpu.VMEM((rows, seq), jnp.float32),
            pltpu.VMEM((rows, columns), jnp.float32),
            dma((3,)),
            dma((kv_heads, 2)),
            dma((heads,)),
            dma((LINE, kv_heads)),
            dma((RINGS * LINE, kv_heads)),
            dma((2, kv_heads)),
            dma((LINE, 2, kv_heads)),
            dma((LINE, kv_heads)),
            dma((LINE + 2, chunks)),
            dma((LINE, chunks)),
            pltpu.SemaphoreType.REGULAR((LINE,)),
        ],
        compiler_params=pltpu.CompilerParams(
            collective_id=variant, has_side_effects=True, vmem_limit_bytes=VMEM_LIMIT
        ),
    )(doc_ids, head_mask, queries, keys, values, w_out)


def fused_device(queries, keys, values, doc_ids, head_mask, w_out):
    operands = (doc_ids, head_mask, queries, keys, values, w_out)
    if len(SLOT_COUNTS) == 1:
        held = fused_call(0, *operands)
    else:
        shift = CHUNK.bit_length() - 1
        at_first = lax.broadcasted_iota(jnp.int32, head_mask.shape, 0) == 0
        offset = jnp.where(at_first, CHUNK - 1 - SLOT_COUNTS[0], 0)
        above = jnp.sum(head_mask + offset)
        which = lax.shift_right_arithmetic(above, jnp.int32(shift))
        held = lax.switch(
            which, [functools.partial(fused_call, i) for i in range(len(SLOT_COUNTS))], *operands
        )
    return pl.pallas_call(
        write_kernel,
        out_shape=jax.ShapeDtypeStruct(held.shape, held.dtype),
        in_specs=[pl.BlockSpec(memory_space=pltpu.VMEM)],
        out_specs=pl.BlockSpec(memory_space=pl.ANY),
        scratch_shapes=[pltpu.SemaphoreType.DMA((4,))],
        compiler_params=pltpu.CompilerParams(vmem_limit_bytes=8 << 20),
    )(held)


def solution(mesh):
    sizes = (mesh.shape["qring"], mesh.shape["kvring"], mesh.shape["head"])
    small = sizes == (RINGS, LINE, 1)
    placed = (
        P(("groups", "qring", "kvring"), "head"),
        P(("groups", "qring", "kvring"), "head"),
        P(("groups", "qring", "kvring"), "head"),
        P("groups"),
        P("head"),
        P("head", "kvring"),
    )
    return jax.shard_map(
        fused_device if small else per_device,
        mesh=mesh,
        in_specs=placed,
        out_specs=P(("groups", "qring", "head"), "kvring"),
        check_vma=False,
    )
```

```python
import functools
import math

import jax
import jax.numpy as jnp
from jax import lax
from jax.experimental import pallas as pl
from jax.experimental.pallas import tpu as pltpu
from jax.sharding import PartitionSpec as P

HD = 128


NEG = -1e30


def block_rows(total_rows, shard_rows):
    best_size = shard_rows
    for multiple in range(1, total_rows // shard_rows + 1):
        if total_rows // shard_rows % multiple == 0 and multiple * shard_rows <= 256:
            best_size = multiple * shard_rows
    return best_size


def attend_keys(state, visible, queries4, key_rows, value_rows, scale_factor):
    run_max, run_sum, run_out = state
    mask4 = visible[:, None, None, :]
    scores = (
        jnp.einsum("rgec,kgc->rgek", queries4, key_rows, preferred_element_type=jnp.float32)
        * scale_factor
    )
    scores = jnp.where(mask4, scores, NEG)
    new_max = jnp.maximum(run_max, jnp.max(scores, axis=-1))
    weights = jnp.where(mask4, jnp.exp(scores - new_max[..., None]), 0.0)
    shrink = jnp.exp(run_max - new_max)
    run_sum = run_sum * shrink + jnp.sum(weights, axis=-1)
    update = jnp.einsum(
        "rgek,kgc->rgec",
        weights.astype(jnp.bfloat16),
        value_rows,
        preferred_element_type=jnp.float32,
    )
    run_out = run_out * shrink[..., None] + update
    return (new_max, run_sum, run_out)


def fold_piece(
    state, pieces, key_start, queries4, query_doc, query_pos, doc_ids, shard_rows, scale_factor
):
    key_all, value_all = pieces
    total_rows = key_all.shape[0]
    block_size = block_rows(total_rows, shard_rows)

    def one_block(index, carry):
        offset = index * block_size
        key_rows = lax.dynamic_slice_in_dim(key_all, offset, block_size, 0)
        value_rows = lax.dynamic_slice_in_dim(value_all, offset, block_size, 0)
        first = key_start + offset
        key_doc = lax.dynamic_slice_in_dim(doc_ids, first, block_size, 0)
        key_pos = first + jnp.arange(block_size, dtype=jnp.int32)
        visible = (query_doc[:, None] == key_doc[None, :]) & (
            key_pos[None, :] <= query_pos[:, None]
        )
        return attend_keys(carry, visible, queries4, key_rows, value_rows, scale_factor)

    return lax.fori_loop(0, total_rows // block_size, one_block, state)


def per_device(queries, keys, values, doc_ids, head_mask, w_out):
    shard_rows = queries.shape[0]
    kv_local = keys.shape[1] // HD
    q_local = queries.shape[1] // HD
    per_group = q_local // kv_local
    scale_factor = 1.0 / math.sqrt(HD)
    cycle_size = lax.axis_size("kvring")
    cycle_index = lax.axis_index("kvring")
    loop_index = lax.axis_index("qring")
    quarter = cycle_size * shard_rows
    key_rows = keys.reshape(shard_rows, kv_local, HD)
    value_rows = values.reshape(shard_rows, kv_local, HD)
    loop_size = lax.axis_size("qring")
    gathered = lax.all_gather(queries, "qring", axis=0, tiled=True)
    query_total = loop_size * shard_rows
    row_ids = jnp.arange(query_total, dtype=jnp.int32)
    query_pos = row_ids // shard_rows * quarter + cycle_index * shard_rows + row_ids % shard_rows
    queries4 = gathered.reshape(query_total, kv_local, per_group, HD)
    query_doc = jnp.take(doc_ids, query_pos)
    key_base = loop_index * quarter
    initial = (
        jnp.full((query_total, kv_local, per_group), NEG, jnp.float32),
        jnp.zeros((query_total, kv_local, per_group), jnp.float32),
        jnp.zeros((query_total, kv_local, per_group, HD), jnp.float32),
    )
    run_max, run_sum, run_out = fold_piece(
        initial,
        (
            lax.all_gather(key_rows, "kvring", axis=0, tiled=True),
            lax.all_gather(value_rows, "kvring", axis=0, tiled=True),
        ),
        key_base,
        queries4,
        query_doc,
        query_pos,
        doc_ids,
        shard_rows,
        scale_factor,
    )
    top = lax.pmax(run_max, "qring")
    factor = jnp.exp(run_max - top)
    numer, denom = (
        lax.psum_scatter(
            (run_out * factor[..., None]).astype(jnp.bfloat16),
            "qring",
            scatter_dimension=0,
            tiled=True,
        ).astype(jnp.float32),
        lax.psum_scatter(
            (run_sum * factor).astype(jnp.bfloat16), "qring", scatter_dimension=0, tiled=True
        ).astype(jnp.float32),
    )
    mask_f = head_mask.reshape(kv_local, per_group).astype(jnp.float32)
    attended = (
        (numer / denom[..., None] * mask_f[None, :, :, None])
        .astype(jnp.bfloat16)
        .reshape(shard_rows, q_local * HD)
    )
    partial_sum = jnp.dot(
        lax.all_gather(attended, "kvring", axis=0, tiled=True),
        w_out,
        preferred_element_type=jnp.float32,
    )
    return lax.psum_scatter(
        partial_sum.astype(jnp.bfloat16), "head", scatter_dimension=0, tiled=True
    )


LINE = 4
RINGS = 4
CHUNK = 2
STACK = 4
RAW = 4
SLOT_COUNTS = (20, 22, 24, 26, 28, 32)
VMEM_LIMIT = 62000000


def fused_kernel(
    slot_count,
    per_group,
    doc_hbm,
    mask_hbm,
    q_hbm,
    k_hbm,
    v_hbm,
    w_hbm,
    o_ref,
    doc_row,
    mask_ref,
    next_ref,
    head_ref,
    q_own,
    q_heads,
    slots,
    kv_all,
    w_all,
    attended,
    bias,
    total,
    local_sem,
    own_sem,
    w_sem,
    kv_send,
    kv_recv,
    kv_pass,
    pass_send,
    mate_send,
    q_send,
    q_recv,
    ready,
):
    z = lax.axis_index("kvring")
    q = lax.axis_index("qring")
    shard = q_hbm.shape[0]
    rows = LINE * shard
    kv_count, _, seq, _ = kv_all.shape
    kv_order = tuple(range(1, kv_count)) + (0,)
    head_count = mask_ref.shape[0]
    width = CHUNK * HD
    chunks = slot_count // CHUNK
    raw = min(RAW, chunks)
    scale2 = math.log2(math.e) / math.sqrt(HD)
    across = lax.rem(q + 2, RINGS)
    mate = q + 1 - 2 * lax.rem(q, 2)
    across_of_mate = lax.rem(mate + 2, RINGS)

    low = q < 2
    high = jnp.logical_not(low)
    even = lax.rem(q, 2) == 0
    quarter = LINE * shard
    upper = z // 2
    sources = (z + 1 - 2 * lax.rem(z, 2), 2 - upper, 3 - 3 * upper)
    middle = (z == 1) | (z == 2)
    end = jnp.logical_not(middle)
    side = sources[0]

    def kv_rows(ring_at, line_at):
        return pl.ds(pl.multiple_of((ring_at * LINE + line_at) * shard, 16), shard)

    def q_rows(line_at):
        return pl.ds(pl.multiple_of(line_at * shard, 16), shard)

    def chunk_cols(c):
        return pl.ds(pl.multiple_of(c * width, 128), width)

    def head_cols(head):
        return pl.ds(pl.multiple_of(head * HD, 128), HD)

    def kv_copy(g, ring_at, line_at, send, target):
        place = kv_all.at[g, :, kv_rows(ring_at, line_at)]
        return pltpu.make_async_remote_copy(
            src_ref=place,
            dst_ref=place,
            send_sem=send.at[g],
            recv_sem=kv_recv.at[ring_at * LINE + line_at, g],
            device_id=target,
            device_id_type=pl.DeviceIdType.MESH,
        )

    def kv_along(g, line_at):
        return kv_copy(g, q, z, kv_send.at[line_at], {"kvring": line_at})

    def kv_arrival(g, ring_at, line_at):
        kv_copy(g, ring_at, line_at, kv_send.at[0], {"kvring": side}).wait_recv()

    def kv_across(g, line_at, place):
        return kv_copy(g, q, line_at, pass_send.at[place, 0], {"qring": across})

    def kv_mate(g, line_at, place):
        return kv_copy(g, q, line_at, pass_send.at[place, 1], {"qring": mate})

    def kv_on(g, line_at, place):
        return kv_copy(g, across, line_at, mate_send.at[place], {"qring": mate})

    def q_copy(line_at, c, kind, target):
        place = slots.at[q_rows(line_at), chunk_cols(c)]
        return pltpu.make_async_remote_copy(
            src_ref=place,
            dst_ref=place,
            send_sem=q_send.at[kind, c],
            recv_sem=q_recv.at[line_at, c],
            device_id={"kvring": target},
            device_id_type=pl.DeviceIdType.MESH,
        )

    def send_chunk(c, line_at):
        q_copy(z, c, line_at, line_at).start()

    def q_arrival(line_at, c):
        q_copy(line_at, c, 0, side).wait_recv()

    def w_copy(head):
        at = pl.ds(pl.multiple_of(head * HD, HD), HD)
        return pltpu.make_async_copy(w_hbm.at[at], w_all.at[head], w_sem.at[head])

    local = [
        pltpu.make_async_copy(mask_hbm, mask_ref, local_sem.at[0]),
        pltpu.make_async_copy(q_hbm, q_own, local_sem.at[1]),
        pltpu.make_async_copy(doc_hbm, doc_row, local_sem.at[2]),
    ]
    own_kv = []
    for g in kv_order:
        for i, own in enumerate((k_hbm, v_hbm)):
            at = kv_all.at[g, i, kv_rows(q, z)]
            own_kv.append(pltpu.make_async_copy(own.at[:, g * HD : (g + 1) * HD], at, own_sem.at[g, i]))

    for copy in own_kv + local:
        copy.start()

    barrier = pltpu.get_barrier_semaphore()
    for step in (1, 2):

        @pl.when(z + step < LINE)
        def _(step=step):
            pl.semaphore_signal(
                barrier, inc=1, device_id={"kvring": z + step}, device_id_type=pl.DeviceIdType.MESH
            )

    for ring_at in (across, mate):
        pl.semaphore_signal(
            barrier, inc=1, device_id={"qring": ring_at}, device_id_type=pl.DeviceIdType.MESH
        )
    pl.semaphore_wait(barrier, jnp.minimum(z, 2) + 2)
    def tell(line_at):
        pl.semaphore_signal(
            ready.at[z], inc=1, device_id={"kvring": line_at}, device_id_type=pl.DeviceIdType.MESH
        )

    @pl.when(z > 0)
    def _():
        tell(z - 1)

    @pl.when(z == 2)
    def _():
        tell(0)

    def down(send):
        @pl.when(z == LINE - 1)
        def _():
            send(z - 2)

        @pl.when(z > 0)
        def _():
            send(z - 1)

    def up(send):
        @pl.when(z == 0)
        def _():
            send(z + 2)

        @pl.when(z < LINE - 1)
        def _():
            send(z + 1)

    def send_kv(line_at):
        for g in kv_order:
            kv_along(g, line_at).start()

    for copy in own_kv:
        copy.wait()
    down(send_kv)

    def pass_on(g, line_at, place):
        @pl.when(low)
        def _():
            kv_across(g, line_at, place).start()

        @pl.when(even)
        def _():
            kv_mate(g, line_at, place).start()

    for g in kv_order:
        pass_on(g, z, 0)

    lag = head_count - slot_count
    local[0].wait()

    later = dropped = jnp.int32(0)
    later = later + head_count
    next_ref[head_count] = later
    for head in reversed(range(head_count)):
        drop = jnp.where(dropped < lag, 1 - mask_ref[head], 0)
        later = head + drop * (later - head)
        dropped = dropped + drop
        next_ref[head] = later
    for s in range(slot_count):
        head_ref[s] = later
        later = next_ref[jnp.minimum(later + 1, head_count)]

    def slot_head(s):
        return jnp.minimum(head_ref[s], head_count - 1)

    def slot_keep(s):
        return mask_ref[slot_head(s)].astype(jnp.float32)

    local[1].wait()
    for head in range(head_count):
        q_heads[head] = q_own[:, head * HD : (head + 1) * HD]

    @pl.loop(0, raw)
    def _(c):
        for e in range(CHUNK):
            s = c * CHUNK + e
            slots[q_rows(z), head_cols(s)] = q_heads[slot_head(s)]

        down(functools.partial(send_chunk, c))

    @pl.when(z < LINE - 1)
    def _():
        pl.semaphore_wait(ready.at[z + 1], 1)
        send_kv(z + 1)

    @pl.when(z == 0)
    def _():
        pl.semaphore_wait(ready.at[2], 1)
        send_kv(2)

    @pl.loop(0, raw)
    def _(c):
        up(functools.partial(send_chunk, c))

    for later in range(1, RINGS):

        @pl.when(q < later)
        def _(later=later):
            at = slice(later * quarter, (later + 1) * quarter)
            kv_all[:, :, at] = jnp.zeros((kv_count, 2, quarter, HD), kv_all.dtype)

    @pl.loop(0, head_count)
    def _(c):
        w_copy(c).start()

    def relay_from(line_at, kind, c):
        @pl.when(middle)
        def _():
            q_arrival(line_at, c)
            q_copy(line_at, c, kind, side).start()

    def relay(i, c):
        relay_from(sources[i], LINE - 1 + i, c)

    def kv_relay(g, place):
        return kv_copy(g, q, sources[place], kv_pass.at[place - 1], {"kvring": side})

    def near(c):
        @pl.when(middle)
        def _():
            q_arrival(side, c)

    def arrive(c):
        @pl.when(end)
        def _():
            for line_at in sources:
                q_arrival(line_at, c)

    places = (z,) + sources

    def kv_from_line(g):
        for place, line_at in enumerate(sources):
            kv_arrival(g, q, line_at)
            if place > 0:

                @pl.when(middle)
                def _(place=place):
                    kv_relay(g, place).start()

            pass_on(g, line_at, place + 1)

    def kv_from_across(g):
        @pl.when(high)
        def _():
            for place, line_at in enumerate(places):
                kv_arrival(g, across, line_at)
                kv_on(g, line_at, place).start()

    def kv_from_mate(g):
        @pl.when(q > 0)
        def _():
            for line_at in places:
                kv_arrival(g, jnp.where(q == 2, 1, 0), line_at)

        @pl.when(q == 3)
        def _():
            for line_at in places:
                kv_arrival(g, mate, line_at)

    local[2].wait()
    row_at = q * rows + lax.broadcasted_iota(jnp.int32, (rows, seq), 0)
    key_at = lax.broadcasted_iota(jnp.int32, (rows, seq), 1)
    key_doc = jnp.broadcast_to(doc_row[...].reshape(1, seq), (rows, seq))
    row_doc = jnp.sum(jnp.where(row_at == key_at, key_doc, 0), axis=1, keepdims=True)
    bias[...] = jnp.where((key_doc == row_doc) & (key_at <= row_at), 0.0, NEG)

    def attend(queries, hidden, key_block, value_block):
        scores = lax.dot_general(
            queries, key_block, (((1,), (1,)), ((), ())), preferred_element_type=jnp.float32
        )
        parts = queries.shape[0] // hidden.shape[0]
        scores = (scores * scale2).reshape(parts, hidden.shape[0], seq) + hidden[None]
        scores = scores.reshape(queries.shape[0], seq)
        top = jnp.max(scores, axis=-1, keepdims=True)
        weights = jnp.exp2(scores - top)
        denom = jnp.sum(weights, axis=-1, keepdims=True)
        context = jnp.dot(
            weights.astype(jnp.bfloat16), value_block, preferred_element_type=jnp.float32
        )
        return context / denom

    def own_stack(g):
        heads = [g * STACK + e for e in range(STACK)]
        stacked = jnp.concatenate([q_heads[head] for head in heads], axis=0)
        kv_head = g * STACK // per_group
        result = attend(stacked, bias[q_rows(z), :], kv_all[kv_head, 0], kv_all[kv_head, 1])
        for e, head in enumerate(heads):
            q_heads[head] = result[e * shard : (e + 1) * shard].astype(jnp.bfloat16)
        for k in range(STACK // CHUNK):
            c = (g * STACK - lag) // CHUNK + k

            @pl.when(c >= raw)
            def _(c=c):
                for e in range(CHUNK):
                    s = c * CHUNK + e
                    block = q_heads[slot_head(s)].astype(jnp.float32) * slot_keep(s)
                    slots[q_rows(z), head_cols(s)] = block.astype(jnp.bfloat16)
                down(functools.partial(send_chunk, c))
                up(functools.partial(send_chunk, c))

    def own_heads(g):
        pl.loop(g * per_group // STACK, (g + 1) * per_group // STACK)(own_stack)

    def kv_at(t):
        return lax.rem(t + 1, kv_count)

    @pl.loop(0, kv_count + 1)
    def _(t):
        @pl.when(t < kv_count)
        def _():
            kv_from_line(kv_at(t))

        @pl.when(t > 0)
        def _():
            kv_from_across(kv_at(t - 1))

        @pl.when((t == 2) | (t == 3))
        def _():
            @pl.loop(0, raw)
            def _(c):
                relay_from(jnp.where(t == 2, sources[1], sources[2]), LINE - 2 + t, c)

        @pl.when(t > 1)
        def _():
            kv_from_mate(kv_at(t - 2))
            own_heads(kv_at(t - 2))

    kv_from_mate(0)

    @pl.loop(0, head_count)
    def _(c):
        w_copy(c).wait()

    def project(block, c, count):
        weights = jnp.concatenate(
            [
                w_all[slot_head(c * CHUNK + e)]
                for e in range(count * CHUNK)
            ],
            axis=0,
        )
        return jnp.dot(block, weights, preferred_element_type=jnp.float32)

    raw_slots = raw * CHUNK
    per_step = -(-(chunks - raw) // raw_slots)

    @pl.loop(0, raw_slots)
    def _(s):
        @pl.when(lax.rem(s, CHUNK) == 0)
        def _():
            arrive(s // CHUNK)
            near(s // CHUNK)

        kv_head = slot_head(s) // per_group
        result = attend(slots[:, head_cols(s)], bias[...], kv_all[kv_head, 0], kv_all[kv_head, 1])
        attended[:, head_cols(s)] = (result * slot_keep(s)).astype(jnp.bfloat16)
        for k in range(per_step):
            ahead = raw + s * per_step + k

            @pl.when(ahead < chunks)
            def _(ahead=ahead):
                relay(1, ahead)

    def wide_cols(c, count):
        return pl.ds(pl.multiple_of(c * width, 128), count * width)

    total[...] = jnp.zeros_like(total)

    @pl.loop(0, raw, step=2)
    def _(c):
        total[...] += project(attended[:, wide_cols(c, 2)], c, 2)

    def take(c, count):
        for k in range(count):
            arrive(c + k)
            near(c + k)
            relay(2, c + k)
        total[...] += project(slots[:, wide_cols(c, count)], c, count)

    odd = (chunks - raw) % 2
    if odd:
        take(raw, 1)

    @pl.loop(0, (chunks - raw - odd) // 2)
    def _(pair):
        take(raw + odd + 2 * pair, 2)

    o_ref[...] = total[...].astype(jnp.bfloat16)

    def sent(line_at):
        for g in kv_order:
            kv_along(g, line_at).wait_send()

        @pl.loop(0, chunks)
        def _(c):
            q_copy(z, c, line_at, line_at).wait_send()

    down(sent)
    up(sent)

    @pl.when(middle)
    def _():
        for place in (1, 2):
            for g in kv_order:
                kv_relay(g, place).wait_send()

            @pl.loop(0, chunks)
            def _(c, place=place):
                q_copy(sources[place], c, LINE - 1 + place, side).wait_send()

    for place, line_at in enumerate(places):
        for g in kv_order:

            @pl.when(low)
            def _(g=g, place=place, line_at=line_at):
                kv_across(g, line_at, place).wait_send()

            @pl.when(even)
            def _(g=g, place=place, line_at=line_at):
                kv_mate(g, line_at, place).wait_send()

            @pl.when(high)
            def _(g=g, place=place, line_at=line_at):
                kv_on(g, line_at, place).wait_send()


def write_kernel(held, out, sem):
    parts = sem.shape[0]
    size = held.shape[0] // parts
    copies = []
    for i in range(parts):
        at = pl.ds(i * size, size)
        copies.append(pltpu.make_async_copy(held.at[at], out.at[at], sem.at[i]))
    for copy in copies:
        copy.start()
    for copy in copies:
        copy.wait()


def fused_call(variant, doc_ids, head_mask, queries, keys, values, w_out):
    slot_count = SLOT_COUNTS[variant]
    shard_rows = queries.shape[0]
    seq = doc_ids.shape[0]
    rows = LINE * shard_rows
    columns = w_out.shape[1]
    heads = head_mask.shape[0]
    chunks = slot_count // CHUNK
    width = CHUNK * HD
    kv_heads = keys.shape[1] // HD
    per_group = heads // kv_heads
    anywhere = pl.BlockSpec(memory_space=pl.ANY)
    dma = pltpu.SemaphoreType.DMA
    return pl.pallas_call(
        functools.partial(fused_kernel, slot_count, per_group),
        out_shape=pltpu.VMEM((rows, columns), jnp.bfloat16),
        in_specs=[anywhere] * 6,
        out_specs=pl.BlockSpec(memory_space=pltpu.VMEM),
        scratch_shapes=[
            pltpu.VMEM((seq,), jnp.int32),
            pltpu.SMEM((heads,), jnp.int32),
            pltpu.SMEM((heads + 1,), jnp.int32),
            pltpu.SMEM((slot_count,), jnp.int32),
            pltpu.VMEM(queries.shape, jnp.bfloat16),
            pltpu.VMEM((heads, shard_rows, HD), jnp.bfloat16),
            pltpu.VMEM((rows, slot_count * HD), jnp.bfloat16),
            pltpu.VMEM((kv_heads, 2, seq, HD), jnp.bfloat16),
            pltpu.VMEM((heads, HD, columns), jnp.bfloat16),
            pltpu.VMEM((rows, min(RAW, chunks) * width), jnp.bfloat16),
            pltpu.VMEM((rows, seq), jnp.float32),
            pltpu.VMEM((rows, columns), jnp.float32),
            dma((3,)),
            dma((kv_heads, 2)),
            dma((heads,)),
            dma((LINE, kv_heads)),
            dma((RINGS * LINE, kv_heads)),
            dma((2, kv_heads)),
            dma((LINE, 2, kv_heads)),
            dma((LINE, kv_heads)),
            dma((LINE + 2, chunks)),
            dma((LINE, chunks)),
            pltpu.SemaphoreType.REGULAR((LINE,)),
        ],
        compiler_params=pltpu.CompilerParams(
            collective_id=variant, has_side_effects=True, vmem_limit_bytes=VMEM_LIMIT
        ),
    )(doc_ids, head_mask, queries, keys, values, w_out)


def fused_device(queries, keys, values, doc_ids, head_mask, w_out):
    operands = (doc_ids, head_mask, queries, keys, values, w_out)
    if len(SLOT_COUNTS) == 1:
        held = fused_call(0, *operands)
    else:
        step = SLOT_COUNTS[1] - SLOT_COUNTS[0]
        at_first = lax.broadcasted_iota(jnp.int32, head_mask.shape, 0) == 0
        offset = jnp.where(at_first, step - 1 - SLOT_COUNTS[0], 0)
        above = jnp.sum(head_mask + offset)
        which = lax.shift_right_arithmetic(above, jnp.int32(step.bit_length() - 1))
        held = lax.switch(
            which, [functools.partial(fused_call, i) for i in range(len(SLOT_COUNTS))], *operands
        )
    return pl.pallas_call(
        write_kernel,
        out_shape=jax.ShapeDtypeStruct(held.shape, held.dtype),
        in_specs=[pl.BlockSpec(memory_space=pltpu.VMEM)],
        out_specs=pl.BlockSpec(memory_space=pl.ANY),
        scratch_shapes=[pltpu.SemaphoreType.DMA((4,))],
        compiler_params=pltpu.CompilerParams(vmem_limit_bytes=8 << 20),
    )(held)


def solution(mesh):
    sizes = (mesh.shape["qring"], mesh.shape["kvring"], mesh.shape["head"])
    small = sizes == (RINGS, LINE, 1)
    placed = (
        P(("groups", "qring", "kvring"), "head"),
        P(("groups", "qring", "kvring"), "head"),
        P(("groups", "qring", "kvring"), "head"),
        P("groups"),
        P("head"),
        P("head", "kvring"),
    )
    return jax.shard_map(
        fused_device if small else per_device,
        mesh=mesh,
        in_specs=placed,
        out_specs=P(("groups", "qring", "head"), "kvring"),
        check_vma=False,
    )
```

```python
import functools
import math

import jax
import jax.numpy as jnp
from jax import lax
from jax.experimental import pallas as pl
from jax.experimental.pallas import tpu as pltpu
from jax.sharding import PartitionSpec as P

HD = 128


NEG = -1e30


def block_rows(total_rows, shard_rows):
    best_size = shard_rows
    for multiple in range(1, total_rows // shard_rows + 1):
        if total_rows // shard_rows % multiple == 0 and multiple * shard_rows <= 256:
            best_size = multiple * shard_rows
    return best_size


def attend_keys(state, visible, queries4, key_rows, value_rows, scale_factor):
    run_max, run_sum, run_out = state
    mask4 = visible[:, None, None, :]
    scores = (
        jnp.einsum("rgec,kgc->rgek", queries4, key_rows, preferred_element_type=jnp.float32)
        * scale_factor
    )
    scores = jnp.where(mask4, scores, NEG)
    new_max = jnp.maximum(run_max, jnp.max(scores, axis=-1))
    weights = jnp.where(mask4, jnp.exp(scores - new_max[..., None]), 0.0)
    shrink = jnp.exp(run_max - new_max)
    run_sum = run_sum * shrink + jnp.sum(weights, axis=-1)
    update = jnp.einsum(
        "rgek,kgc->rgec",
        weights.astype(jnp.bfloat16),
        value_rows,
        preferred_element_type=jnp.float32,
    )
    run_out = run_out * shrink[..., None] + update
    return (new_max, run_sum, run_out)


def fold_piece(
    state, pieces, key_start, queries4, query_doc, query_pos, doc_ids, shard_rows, scale_factor
):
    key_all, value_all = pieces
    total_rows = key_all.shape[0]
    block_size = block_rows(total_rows, shard_rows)

    def one_block(index, carry):
        offset = index * block_size
        key_rows = lax.dynamic_slice_in_dim(key_all, offset, block_size, 0)
        value_rows = lax.dynamic_slice_in_dim(value_all, offset, block_size, 0)
        first = key_start + offset
        key_doc = lax.dynamic_slice_in_dim(doc_ids, first, block_size, 0)
        key_pos = first + jnp.arange(block_size, dtype=jnp.int32)
        visible = (query_doc[:, None] == key_doc[None, :]) & (
            key_pos[None, :] <= query_pos[:, None]
        )
        return attend_keys(carry, visible, queries4, key_rows, value_rows, scale_factor)

    return lax.fori_loop(0, total_rows // block_size, one_block, state)


def per_device(queries, keys, values, doc_ids, head_mask, w_out):
    shard_rows = queries.shape[0]
    kv_local = keys.shape[1] // HD
    q_local = queries.shape[1] // HD
    per_group = q_local // kv_local
    scale_factor = 1.0 / math.sqrt(HD)
    cycle_size = lax.axis_size("kvring")
    cycle_index = lax.axis_index("kvring")
    loop_index = lax.axis_index("qring")
    quarter = cycle_size * shard_rows
    key_rows = keys.reshape(shard_rows, kv_local, HD)
    value_rows = values.reshape(shard_rows, kv_local, HD)
    loop_size = lax.axis_size("qring")
    gathered = lax.all_gather(queries, "qring", axis=0, tiled=True)
    query_total = loop_size * shard_rows
    row_ids = jnp.arange(query_total, dtype=jnp.int32)
    query_pos = row_ids // shard_rows * quarter + cycle_index * shard_rows + row_ids % shard_rows
    queries4 = gathered.reshape(query_total, kv_local, per_group, HD)
    query_doc = jnp.take(doc_ids, query_pos)
    key_base = loop_index * quarter
    initial = (
        jnp.full((query_total, kv_local, per_group), NEG, jnp.float32),
        jnp.zeros((query_total, kv_local, per_group), jnp.float32),
        jnp.zeros((query_total, kv_local, per_group, HD), jnp.float32),
    )
    run_max, run_sum, run_out = fold_piece(
        initial,
        (
            lax.all_gather(key_rows, "kvring", axis=0, tiled=True),
            lax.all_gather(value_rows, "kvring", axis=0, tiled=True),
        ),
        key_base,
        queries4,
        query_doc,
        query_pos,
        doc_ids,
        shard_rows,
        scale_factor,
    )
    top = lax.pmax(run_max, "qring")
    factor = jnp.exp(run_max - top)
    numer, denom = (
        lax.psum_scatter(
            (run_out * factor[..., None]).astype(jnp.bfloat16),
            "qring",
            scatter_dimension=0,
            tiled=True,
        ).astype(jnp.float32),
        lax.psum_scatter(
            (run_sum * factor).astype(jnp.bfloat16), "qring", scatter_dimension=0, tiled=True
        ).astype(jnp.float32),
    )
    mask_f = head_mask.reshape(kv_local, per_group).astype(jnp.float32)
    attended = (
        (numer / denom[..., None] * mask_f[None, :, :, None])
        .astype(jnp.bfloat16)
        .reshape(shard_rows, q_local * HD)
    )
    partial_sum = jnp.dot(
        lax.all_gather(attended, "kvring", axis=0, tiled=True),
        w_out,
        preferred_element_type=jnp.float32,
    )
    return lax.psum_scatter(
        partial_sum.astype(jnp.bfloat16), "head", scatter_dimension=0, tiled=True
    )


LINE = 4
RINGS = 4
CHUNK = 2
STACK = 8
RAW = 4
SLOT_COUNTS = (20, 22, 24, 26, 28, 32)
VMEM_LIMIT = 62000000


def fused_kernel(
    slot_count,
    per_group,
    doc_hbm,
    mask_hbm,
    q_hbm,
    k_hbm,
    v_hbm,
    w_hbm,
    o_ref,
    doc_row,
    mask_ref,
    next_ref,
    head_ref,
    q_own,
    q_heads,
    slots,
    kv_all,
    w_all,
    attended,
    bias,
    total,
    local_sem,
    own_sem,
    w_sem,
    kv_send,
    kv_recv,
    kv_pass,
    pass_send,
    mate_send,
    q_send,
    q_recv,
    ready,
):
    z = lax.axis_index("kvring")
    q = lax.axis_index("qring")
    shard = q_hbm.shape[0]
    rows = LINE * shard
    kv_count, _, seq, _ = kv_all.shape
    kv_order = tuple(range(1, kv_count)) + (0,)
    head_count = mask_ref.shape[0]
    width = CHUNK * HD
    chunks = slot_count // CHUNK
    raw = min(RAW, chunks)
    scale2 = math.log2(math.e) / math.sqrt(HD)
    across = lax.rem(q + 2, RINGS)
    mate = q + 1 - 2 * lax.rem(q, 2)
    across_of_mate = lax.rem(mate + 2, RINGS)

    low = q < 2
    high = jnp.logical_not(low)
    even = lax.rem(q, 2) == 0
    quarter = LINE * shard
    upper = z // 2
    sources = (z + 1 - 2 * lax.rem(z, 2), 2 - upper, 3 - 3 * upper)
    middle = (z == 1) | (z == 2)
    end = jnp.logical_not(middle)
    side = sources[0]

    def kv_rows(ring_at, line_at):
        return pl.ds(pl.multiple_of((ring_at * LINE + line_at) * shard, 16), shard)

    def q_rows(line_at):
        return pl.ds(pl.multiple_of(line_at * shard, 16), shard)

    def chunk_cols(c):
        return pl.ds(pl.multiple_of(c * width, 128), width)

    def head_cols(head):
        return pl.ds(pl.multiple_of(head * HD, 128), HD)

    def kv_copy(g, ring_at, line_at, send, target):
        place = kv_all.at[g, :, kv_rows(ring_at, line_at)]
        return pltpu.make_async_remote_copy(
            src_ref=place,
            dst_ref=place,
            send_sem=send.at[g],
            recv_sem=kv_recv.at[ring_at * LINE + line_at, g],
            device_id=target,
            device_id_type=pl.DeviceIdType.MESH,
        )

    def kv_along(g, line_at):
        return kv_copy(g, q, z, kv_send.at[line_at], {"kvring": line_at})

    def kv_arrival(g, ring_at, line_at):
        kv_copy(g, ring_at, line_at, kv_send.at[0], {"kvring": side}).wait_recv()

    def kv_across(g, line_at, place):
        return kv_copy(g, q, line_at, pass_send.at[place, 0], {"qring": across})

    def kv_mate(g, line_at, place):
        return kv_copy(g, q, line_at, pass_send.at[place, 1], {"qring": mate})

    def kv_on(g, line_at, place):
        return kv_copy(g, across, line_at, mate_send.at[place], {"qring": mate})

    def q_copy(line_at, c, kind, target):
        place = slots.at[q_rows(line_at), chunk_cols(c)]
        return pltpu.make_async_remote_copy(
            src_ref=place,
            dst_ref=place,
            send_sem=q_send.at[kind, c],
            recv_sem=q_recv.at[line_at, c],
            device_id={"kvring": target},
            device_id_type=pl.DeviceIdType.MESH,
        )

    def send_chunk(c, line_at):
        q_copy(z, c, line_at, line_at).start()

    def q_arrival(line_at, c):
        q_copy(line_at, c, 0, side).wait_recv()

    def w_copy(head):
        at = pl.ds(pl.multiple_of(head * HD, HD), HD)
        return pltpu.make_async_copy(w_hbm.at[at], w_all.at[head], w_sem.at[head])

    local = [
        pltpu.make_async_copy(mask_hbm, mask_ref, local_sem.at[0]),
        pltpu.make_async_copy(q_hbm, q_own, local_sem.at[1]),
        pltpu.make_async_copy(doc_hbm, doc_row, local_sem.at[2]),
    ]
    own_kv = []
    for g in kv_order:
        for i, own in enumerate((k_hbm, v_hbm)):
            at = kv_all.at[g, i, kv_rows(q, z)]
            own_kv.append(pltpu.make_async_copy(own.at[:, g * HD : (g + 1) * HD], at, own_sem.at[g, i]))

    for copy in own_kv + local:
        copy.start()

    barrier = pltpu.get_barrier_semaphore()
    for step in (1, 2):

        @pl.when(z + step < LINE)
        def _(step=step):
            pl.semaphore_signal(
                barrier, inc=1, device_id={"kvring": z + step}, device_id_type=pl.DeviceIdType.MESH
            )

    for ring_at in (across, mate):
        pl.semaphore_signal(
            barrier, inc=1, device_id={"qring": ring_at}, device_id_type=pl.DeviceIdType.MESH
        )
    pl.semaphore_wait(barrier, jnp.minimum(z, 2) + 2)
    def tell(line_at):
        pl.semaphore_signal(
            ready.at[z], inc=1, device_id={"kvring": line_at}, device_id_type=pl.DeviceIdType.MESH
        )

    @pl.when(z > 0)
    def _():
        tell(z - 1)

    @pl.when(z == 2)
    def _():
        tell(0)

    def down(send):
        @pl.when(z == LINE - 1)
        def _():
            send(z - 2)

        @pl.when(z > 0)
        def _():
            send(z - 1)

    def up(send):
        @pl.when(z == 0)
        def _():
            send(z + 2)

        @pl.when(z < LINE - 1)
        def _():
            send(z + 1)

    def send_kv(line_at):
        for g in kv_order:
            kv_along(g, line_at).start()

    for copy in own_kv:
        copy.wait()
    down(send_kv)

    def pass_on(g, line_at, place):
        @pl.when(low)
        def _():
            kv_across(g, line_at, place).start()

        @pl.when(even)
        def _():
            kv_mate(g, line_at, place).start()

    for g in kv_order:
        pass_on(g, z, 0)

    lag = head_count - slot_count
    local[0].wait()

    later = dropped = jnp.int32(0)
    later = later + head_count
    next_ref[head_count] = later
    for head in reversed(range(head_count)):
        drop = jnp.where(dropped < lag, 1 - mask_ref[head], 0)
        later = head + drop * (later - head)
        dropped = dropped + drop
        next_ref[head] = later
    for s in range(slot_count):
        head_ref[s] = later
        later = next_ref[jnp.minimum(later + 1, head_count)]

    def slot_head(s):
        return jnp.minimum(head_ref[s], head_count - 1)

    def slot_keep(s):
        return mask_ref[slot_head(s)].astype(jnp.float32)

    local[1].wait()
    for head in range(head_count):
        q_heads[head] = q_own[:, head * HD : (head + 1) * HD]

    @pl.loop(0, raw)
    def _(c):
        for e in range(CHUNK):
            s = c * CHUNK + e
            slots[q_rows(z), head_cols(s)] = q_heads[slot_head(s)]

        down(functools.partial(send_chunk, c))

    @pl.when(z < LINE - 1)
    def _():
        pl.semaphore_wait(ready.at[z + 1], 1)
        send_kv(z + 1)

    @pl.when(z == 0)
    def _():
        pl.semaphore_wait(ready.at[2], 1)
        send_kv(2)

    @pl.loop(0, raw)
    def _(c):
        up(functools.partial(send_chunk, c))

    for later in range(1, RINGS):

        @pl.when(q < later)
        def _(later=later):
            at = slice(later * quarter, (later + 1) * quarter)
            kv_all[:, :, at] = jnp.zeros((kv_count, 2, quarter, HD), kv_all.dtype)

    @pl.loop(0, head_count)
    def _(c):
        w_copy(c).start()

    def relay_from(line_at, kind, c):
        @pl.when(middle)
        def _():
            q_arrival(line_at, c)
            q_copy(line_at, c, kind, side).start()

    def relay(i, c):
        relay_from(sources[i], LINE - 1 + i, c)

    def kv_relay(g, place):
        return kv_copy(g, q, sources[place], kv_pass.at[place - 1], {"kvring": side})

    def near(c):
        @pl.when(middle)
        def _():
            q_arrival(side, c)

    def arrive(c):
        @pl.when(end)
        def _():
            for line_at in sources:
                q_arrival(line_at, c)

    places = (z,) + sources

    def kv_from_line(g):
        for place, line_at in enumerate(sources):
            kv_arrival(g, q, line_at)
            if place > 0:

                @pl.when(middle)
                def _(place=place):
                    kv_relay(g, place).start()

            pass_on(g, line_at, place + 1)

    def kv_from_across(g):
        @pl.when(high)
        def _():
            for place, line_at in enumerate(places):
                kv_arrival(g, across, line_at)
                kv_on(g, line_at, place).start()

    def kv_from_mate(g):
        @pl.when(q > 0)
        def _():
            for line_at in places:
                kv_arrival(g, jnp.where(q == 2, 1, 0), line_at)

        @pl.when(q == 3)
        def _():
            for line_at in places:
                kv_arrival(g, mate, line_at)

    local[2].wait()
    row_at = q * rows + lax.broadcasted_iota(jnp.int32, (rows, seq), 0)
    key_at = lax.broadcasted_iota(jnp.int32, (rows, seq), 1)
    key_doc = jnp.broadcast_to(doc_row[...].reshape(1, seq), (rows, seq))
    row_doc = jnp.sum(jnp.where(row_at == key_at, key_doc, 0), axis=1, keepdims=True)
    bias[...] = jnp.where((key_doc == row_doc) & (key_at <= row_at), 0.0, NEG)

    def attend(queries, hidden, key_block, value_block):
        scores = lax.dot_general(
            queries, key_block, (((1,), (1,)), ((), ())), preferred_element_type=jnp.float32
        )
        parts = queries.shape[0] // hidden.shape[0]
        scores = (scores * scale2).reshape(parts, hidden.shape[0], seq) + hidden[None]
        scores = scores.reshape(queries.shape[0], seq)
        top = jnp.max(scores, axis=-1, keepdims=True)
        weights = jnp.exp2(scores - top)
        denom = jnp.sum(weights, axis=-1, keepdims=True)
        context = jnp.dot(
            weights.astype(jnp.bfloat16), value_block, preferred_element_type=jnp.float32
        )
        return context / denom

    def own_stack(g):
        heads = [g * STACK + e for e in range(STACK)]
        stacked = jnp.concatenate([q_heads[head] for head in heads], axis=0)
        kv_head = g * STACK // per_group
        result = attend(stacked, bias[q_rows(z), :], kv_all[kv_head, 0], kv_all[kv_head, 1])
        for e, head in enumerate(heads):
            q_heads[head] = result[e * shard : (e + 1) * shard].astype(jnp.bfloat16)
        for k in range(STACK // CHUNK):
            c = (g * STACK - lag) // CHUNK + k

            @pl.when(c >= raw)
            def _(c=c):
                for e in range(CHUNK):
                    s = c * CHUNK + e
                    block = q_heads[slot_head(s)].astype(jnp.float32) * slot_keep(s)
                    slots[q_rows(z), head_cols(s)] = block.astype(jnp.bfloat16)
                down(functools.partial(send_chunk, c))
                up(functools.partial(send_chunk, c))

    def own_heads(g):
        pl.loop(g * per_group // STACK, (g + 1) * per_group // STACK)(own_stack)

    def kv_at(t):
        return lax.rem(t + 1, kv_count)

    @pl.loop(0, kv_count + 1)
    def _(t):
        @pl.when(t < kv_count)
        def _():
            kv_from_line(kv_at(t))

        @pl.when(t > 0)
        def _():
            kv_from_across(kv_at(t - 1))

        @pl.when((t == 2) | (t == 3))
        def _():
            @pl.loop(0, raw)
            def _(c):
                relay_from(jnp.where(t == 2, sources[1], sources[2]), LINE - 2 + t, c)

        @pl.when(t > 1)
        def _():
            kv_from_mate(kv_at(t - 2))
            own_heads(kv_at(t - 2))

    kv_from_mate(0)

    @pl.loop(0, head_count)
    def _(c):
        w_copy(c).wait()

    def project(block, c, count):
        weights = jnp.concatenate(
            [
                w_all[slot_head(c * CHUNK + e)]
                for e in range(count * CHUNK)
            ],
            axis=0,
        )
        return jnp.dot(block, weights, preferred_element_type=jnp.float32)

    raw_slots = raw * CHUNK
    per_step = -(-(chunks - raw) // raw_slots)

    @pl.loop(0, raw_slots)
    def _(s):
        @pl.when(lax.rem(s, CHUNK) == 0)
        def _():
            arrive(s // CHUNK)
            near(s // CHUNK)

        kv_head = slot_head(s) // per_group
        result = attend(slots[:, head_cols(s)], bias[...], kv_all[kv_head, 0], kv_all[kv_head, 1])
        attended[:, head_cols(s)] = (result * slot_keep(s)).astype(jnp.bfloat16)
        for k in range(per_step):
            ahead = raw + s * per_step + k

            @pl.when(ahead < chunks)
            def _(ahead=ahead):
                relay(1, ahead)

    def wide_cols(c, count):
        return pl.ds(pl.multiple_of(c * width, 128), count * width)

    total[...] = project(attended[...], 0, raw)

    def take(c, count, into=total):
        for k in range(count):
            arrive(c + k)
            near(c + k)
            relay(2, c + k)
        fresh = project(slots[:, wide_cols(c, count)], c, count)
        into[...] = (total[...] + fresh).astype(into.dtype)

    odd = (chunks - raw) % 2
    if odd:
        take(raw, 1)

    @pl.loop(0, (chunks - raw - odd) // 2 - 1)
    def _(pair):
        take(raw + odd + 2 * pair, 2)

    take(chunks - 2, 2, o_ref)

    def sent(line_at):
        for g in kv_order:
            kv_along(g, line_at).wait_send()

        @pl.loop(0, chunks)
        def _(c):
            q_copy(z, c, line_at, line_at).wait_send()

    down(sent)
    up(sent)

    @pl.when(middle)
    def _():
        for place in (1, 2):
            for g in kv_order:
                kv_relay(g, place).wait_send()

            @pl.loop(0, chunks)
            def _(c, place=place):
                q_copy(sources[place], c, LINE - 1 + place, side).wait_send()

    for place, line_at in enumerate(places):
        for g in kv_order:

            @pl.when(low)
            def _(g=g, place=place, line_at=line_at):
                kv_across(g, line_at, place).wait_send()

            @pl.when(even)
            def _(g=g, place=place, line_at=line_at):
                kv_mate(g, line_at, place).wait_send()

            @pl.when(high)
            def _(g=g, place=place, line_at=line_at):
                kv_on(g, line_at, place).wait_send()


def write_kernel(held, out, sem):
    parts = sem.shape[0]
    size = held.shape[0] // parts
    copies = []
    for i in range(parts):
        at = pl.ds(i * size, size)
        copies.append(pltpu.make_async_copy(held.at[at], out.at[at], sem.at[i]))
    for copy in copies:
        copy.start()
    for copy in copies:
        copy.wait()


def fused_call(variant, doc_ids, head_mask, queries, keys, values, w_out):
    slot_count = SLOT_COUNTS[variant]
    shard_rows = queries.shape[0]
    seq = doc_ids.shape[0]
    rows = LINE * shard_rows
    columns = w_out.shape[1]
    heads = head_mask.shape[0]
    chunks = slot_count // CHUNK
    width = CHUNK * HD
    kv_heads = keys.shape[1] // HD
    per_group = heads // kv_heads
    anywhere = pl.BlockSpec(memory_space=pl.ANY)
    dma = pltpu.SemaphoreType.DMA
    return pl.pallas_call(
        functools.partial(fused_kernel, slot_count, per_group),
        out_shape=pltpu.VMEM((rows, columns), jnp.bfloat16),
        in_specs=[anywhere] * 6,
        out_specs=pl.BlockSpec(memory_space=pltpu.VMEM),
        scratch_shapes=[
            pltpu.VMEM((seq,), jnp.int32),
            pltpu.SMEM((heads,), jnp.int32),
            pltpu.SMEM((heads + 1,), jnp.int32),
            pltpu.SMEM((slot_count,), jnp.int32),
            pltpu.VMEM(queries.shape, jnp.bfloat16),
            pltpu.VMEM((heads, shard_rows, HD), jnp.bfloat16),
            pltpu.VMEM((rows, slot_count * HD), jnp.bfloat16),
            pltpu.VMEM((kv_heads, 2, seq, HD), jnp.bfloat16),
            pltpu.VMEM((heads, HD, columns), jnp.bfloat16),
            pltpu.VMEM((rows, min(RAW, chunks) * width), jnp.bfloat16),
            pltpu.VMEM((rows, seq), jnp.float32),
            pltpu.VMEM((rows, columns), jnp.float32),
            dma((3,)),
            dma((kv_heads, 2)),
            dma((heads,)),
            dma((LINE, kv_heads)),
            dma((RINGS * LINE, kv_heads)),
            dma((2, kv_heads)),
            dma((LINE, 2, kv_heads)),
            dma((LINE, kv_heads)),
            dma((LINE + 2, chunks)),
            dma((LINE, chunks)),
            pltpu.SemaphoreType.REGULAR((LINE,)),
        ],
        compiler_params=pltpu.CompilerParams(
            collective_id=variant, has_side_effects=True, vmem_limit_bytes=VMEM_LIMIT
        ),
    )(doc_ids, head_mask, queries, keys, values, w_out)


def fused_device(queries, keys, values, doc_ids, head_mask, w_out):
    operands = (doc_ids, head_mask, queries, keys, values, w_out)
    if len(SLOT_COUNTS) == 1:
        held = fused_call(0, *operands)
    else:
        step = SLOT_COUNTS[1] - SLOT_COUNTS[0]
        at_first = lax.broadcasted_iota(jnp.int32, head_mask.shape, 0) == 0
        offset = jnp.where(at_first, step - 1 - SLOT_COUNTS[0], 0)
        above = jnp.sum(head_mask + offset)
        which = lax.shift_right_arithmetic(above, jnp.int32(step.bit_length() - 1))
        held = lax.switch(
            which, [functools.partial(fused_call, i) for i in range(len(SLOT_COUNTS))], *operands
        )
    return pl.pallas_call(
        write_kernel,
        out_shape=jax.ShapeDtypeStruct(held.shape, held.dtype),
        in_specs=[pl.BlockSpec(memory_space=pltpu.VMEM)],
        out_specs=pl.BlockSpec(memory_space=pl.ANY),
        scratch_shapes=[pltpu.SemaphoreType.DMA((4,))],
        compiler_params=pltpu.CompilerParams(vmem_limit_bytes=8 << 20),
    )(held)


def solution(mesh):
    sizes = (mesh.shape["qring"], mesh.shape["kvring"], mesh.shape["head"])
    small = sizes == (RINGS, LINE, 1)
    placed = (
        P(("groups", "qring", "kvring"), "head"),
        P(("groups", "qring", "kvring"), "head"),
        P(("groups", "qring", "kvring"), "head"),
        P("groups"),
        P("head"),
        P("head", "kvring"),
    )
    return jax.shard_map(
        fused_device if small else per_device,
        mesh=mesh,
        in_specs=placed,
        out_specs=P(("groups", "qring", "head"), "kvring"),
        check_vma=False,
    )
```
